128 devices in a mesh: grp: 4 (over z_lo, core), dev: 32 (over x, y, z_hi).
Axes of the slice: x: 4, y: 4, z: 4 (z_hi: 2, z_lo: 2; z = z_hi * 2 + z_lo), core: 2. Of those that a mesh axis runs over, the one named last changes fastest.
Arguments:
- dosage: bfloat16 [2048, 131072], P('dev', 'grp'), may hold values from 0 to 2
- variant_slot: int32 [1024], replicated, may hold values from 0 to 2047, as said below
- center: float32 [1024], replicated, may hold values from 0.5 to 1.5
- variant_scale: float32 [1024], replicated, may hold values from 0.3 to 3
- sample_signs: int32 [131072], P(('grp', 'dev')), may hold values from -1 to 1, as said below
- sample_perm: int32 [131072], P(('grp', 'dev')), may hold values from 0 to 131071, as said below
- sample_rows: int32 [4096], P(('grp', 'dev')), may hold values from 0 to 131071, as said below
- projection: bfloat16 [1024, 256], replicated, may hold values from -0.1875 to 0.1875
Outputs:
- sketch: float32 [4096, 256], P(('grp', 'dev'))
The draws below stay inside these ranges and needn't reach their ends.
Inputs may be any that keep to these rules, and one draw needn't show every extreme that they name: `variant_slot`: each slot holds at most one variant; file f holds its variants in its first slots; the last file, 31, is full with 64 variants; every other file holds at most 32. `sample_signs`: each value is -1 or +1. `sample_perm`: a permutation that maps each aligned block of 1024 positions onto the same block. `sample_rows`: rows m with the same m // 32 = b hold distinct positions of block b, between b * 1024 and (b + 1) * 1024 - 1.
All inputs are finite; a program needn't handle non-finite values.
Results may differ from the reference program's by a relative error of at most 0.0091.
Values may be sent and summed in bfloat16 or wider, within the bound.
No kernel may reach another device: no remote copies, remote signals or barrier semaphores. Data moves between devices by JAX's collectives and lax.ppermute only.
A program may use at most 64 MiB of HBM per device.

```python
import math
import jax
import jax.numpy as jnp
from jax import lax

V = 1024
K = 256
SAMP_DEV = 1024
ROWS_DEV = 32
FILES = 32
FILE_CAP = 64
SAMPLES = 131072
SKETCH_ROWS = 4096


def draw_variant_slot(key, part):
    second_key = jax.random.fold_in(jax.random.fold_in(key, 7), 1)
    full_file = FILES - 1
    file_ids = jnp.arange(FILES, dtype=jnp.int32)
    file_order = (file_ids - full_file - 1) % FILES
    remaining = V - FILE_CAP
    base_count = remaining // (FILES - 1)
    extra_count = remaining % (FILES - 1)
    counts = jnp.where(file_ids == full_file, FILE_CAP, base_count + (file_order < extra_count).astype(jnp.int32))
    file_ends = jnp.cumsum(counts).astype(jnp.int32)
    file_starts = file_ends - counts
    positions = jnp.arange(V, dtype=jnp.int32)
    owner_file = jnp.sum((file_ends[None, :] <= positions[:, None]).astype(jnp.int32), axis=1)
    within_file = positions - file_starts[owner_file]
    slot_of_position = (owner_file * FILE_CAP + within_file).astype(jnp.int32)
    shuffled = jax.random.permutation(second_key, V).astype(jnp.int32)
    return jnp.zeros((V,), jnp.int32).at[shuffled].set(slot_of_position)


def draw_sample_signs(key, part):
    return (2 * jax.random.randint(jax.random.fold_in(key, 11), (SAMPLES,), 0, 2) - 1).astype(jnp.int32)


def draw_sample_perm(key, part):
    block_keys = jax.random.split(jax.random.fold_in(key, 13), SAMPLES // SAMP_DEV)
    blocks = jax.vmap(lambda block_key: jax.random.permutation(block_key, SAMP_DEV).astype(jnp.int32))(block_keys)
    offsets = (jnp.arange(SAMPLES // SAMP_DEV, dtype=jnp.int32) * SAMP_DEV)[:, None]
    return (blocks + offsets).reshape(SAMPLES).astype(jnp.int32)


def draw_sample_rows(key, part):
    block_count = SKETCH_ROWS // ROWS_DEV
    block_keys = jax.random.split(jax.random.fold_in(key, 17), block_count)
    blocks = jax.vmap(lambda block_key: jax.random.permutation(block_key, SAMP_DEV)[:ROWS_DEV].astype(jnp.int32))(block_keys)
    block_ids = jnp.arange(block_count, dtype=jnp.int32)
    leading = blocks[:, 0]
    shift_by = jnp.where(block_ids == 0, -leading, jnp.where(block_ids == block_count - 1, SAMP_DEV - 1 - leading, 0)).astype(jnp.int32)
    blocks = ((blocks + shift_by[:, None]) % SAMP_DEV).astype(jnp.int32)
    offsets = (block_ids * SAMP_DEV)[:, None]
    return (blocks + offsets).reshape(SKETCH_ROWS).astype(jnp.int32)


def levels(key, shape, pieces, least, largest):
    factor_of, own = 1.0, jax.random.fold_in(key, 6)
    for position, blocks in pieces:
        heights = jnp.exp(jax.random.uniform(jax.random.fold_in(own, position), (blocks,), jnp.float32, least / len(pieces), largest / len(pieces)))
        factor_of = factor_of * jnp.repeat(heights, shape[position] // blocks).reshape([-1 if axis == position else 1 for axis in range(len(shape))])
    return factor_of


def normal_values(rng, dims, width, reach, kind=jnp.bfloat16):
    result = jax.random.normal(rng, dims, jnp.float32) * width
    return jnp.minimum(jnp.maximum(result, -reach), reach).astype(kind)


def setup_inputs(seed: int = 0) -> dict:
    streams_of = jax.random.split(jax.random.key(seed), 9)
    dosage = jnp.clip(2.0 * jax.random.uniform(streams_of[0], (FILES * FILE_CAP, SAMPLES), jnp.float32) ** levels(streams_of[0], (FILES * FILE_CAP, SAMPLES), ((0, 32), (1, 4)), -0.2, 0.2), 0.0, 2.0).astype(jnp.bfloat16)
    variant_slot = draw_variant_slot(jax.random.fold_in(streams_of[8], 71), 0)
    center = jnp.clip(jax.random.uniform(streams_of[2], (V,), jnp.float32, 0.5, 1.5), 0.5, 1.5)
    variant_scale = jnp.clip(jnp.exp(jax.random.uniform(streams_of[3], (V,), jnp.float32, math.log(0.3), math.log(3.0))), 0.3, 3.0)
    sample_signs = draw_sample_signs(jax.random.fold_in(streams_of[8], 71), 0)
    sample_perm = draw_sample_perm(jax.random.fold_in(streams_of[8], 71), 0)
    sample_rows = draw_sample_rows(jax.random.fold_in(streams_of[8], 71), 0)
    projection = normal_values(streams_of[7], (V, K), V ** -0.5, 0.1875)
    return {"dosage": dosage, "variant_slot": variant_slot, "center": center, "variant_scale": variant_scale, "sample_signs": sample_signs, "sample_perm": sample_perm, "sample_rows": sample_rows, "projection": projection}


root_half = 0.7071067811865476

def butterfly(values, stride):
    viewed = values.reshape(values.shape[0], -1, 2, stride)
    first_half = viewed[:, :, 0]
    second_half = viewed[:, :, 1]
    return jnp.stack([first_half + second_half, first_half - second_half], axis=2).reshape(values.shape)

def reference(dosage, variant_slot, center, variant_scale, sample_signs, sample_perm, sample_rows, projection):
    genotype = jnp.take(dosage, variant_slot, axis=0)
    genotype = jnp.take(genotype, sample_perm, axis=1)
    signed = ((genotype.astype(jnp.float32) - center[:, None]) * variant_scale[:, None] * sample_signs.astype(jnp.float32)[None, :]).astype(jnp.bfloat16)
    projected = lax.dot_general(projection, signed, (((0,), (0,)), ((), ())), preferred_element_type=jnp.float32).astype(jnp.bfloat16)
    mixed_data = projected.astype(jnp.float32)
    stride = 1
    while stride < SAMP_DEV:
        mixed_data = butterfly(mixed_data, stride)
        stride = stride * 2
    mixed_data = (mixed_data * (1.0 / math.sqrt(SAMP_DEV))).astype(jnp.bfloat16)
    while stride < SAMPLES:
        mixed_data = (butterfly(mixed_data.astype(jnp.float32), stride) * root_half).astype(jnp.bfloat16)
        stride = stride * 2
    picked = jnp.take(mixed_data, sample_rows, axis=1)
    return jnp.transpose(picked).astype(jnp.float32)
```

```python
import math

import jax
import jax.numpy as jnp
from jax import lax
from jax.experimental import pallas as pl
from jax.experimental.pallas import tpu as pltpu
from jax.sharding import PartitionSpec as P

V = 1024
K = 256
SECTION = 1024
LOW = 256
HIGH = SECTION // LOW
CAP = 64
BF = jnp.bfloat16
F32 = jnp.float32


def iota(shape, axis):
    return lax.broadcasted_iota(jnp.int32, shape, axis)


def parity_sign(bits):
    bits = bits ^ (bits >> 4)
    bits = bits ^ (bits >> 2)
    bits = bits ^ (bits >> 1)
    return (1 - 2 * (bits & 1)).astype(F32)


def invert_kernel(perm_ref, sign_ref, out_ref):
    spot = perm_ref[...] & (SECTION - 1)
    where_is = (jnp.broadcast_to(spot, (SECTION, SECTION)) == iota((SECTION, SECTION), 0)).astype(F32).astype(BF)
    position = iota((8, SECTION), 1)
    negative = jnp.broadcast_to((sign_ref[...] < 0).astype(jnp.int32), (8, SECTION))
    digits = jnp.where(iota((8, SECTION), 0) == 0, position % LOW, position // LOW + HIGH * negative)
    found = lax.dot_general(digits.astype(F32).astype(BF), where_is, (((1,), (1,)), ((), ())), preferred_element_type=F32)
    found = found.astype(jnp.int32)
    out_ref[...] = found[0:1] + LOW * found[1:2]


def slot_kernel(slot_ref, proj_ref, out_ref):
    slot = slot_ref[...]
    target = (slot // 16 % 4) * 512 + slot // CAP * 16 + slot % 16
    chunk = 512
    proj = proj_ref[...]
    for c in range(4):
        hot = (jnp.broadcast_to(target, (chunk, V)) == iota((chunk, V), 0) + c * chunk).astype(F32).astype(BF)
        out_ref[c] = jnp.dot(hot, proj, preferred_element_type=F32).astype(BF)


def mix_kernel(place_ref, dos_hbm, code_ref, rows_ref, slot_ref, cen_ref, scl_ref, out_ref, dos, mix, sems):
    blocks = dos.shape[0]

    def fetch(b):
        return pltpu.make_async_copy(dos_hbm.at[:, pl.ds(b * SECTION, SECTION)], dos.at[b], sems.at[b])

    for b in range(blocks):
        fetch(b).start()

    mine = jnp.broadcast_to(slot_ref[...], (CAP, V)) == iota((CAP, V), 0) + place_ref[0] * CAP
    center = jnp.sum(jnp.where(mine, jnp.broadcast_to(cen_ref[...], (CAP, V)), 0.0), axis=1, keepdims=True)
    scale = jnp.sum(jnp.where(mine, jnp.broadcast_to(scl_ref[...], (CAP, V)), 0.0), axis=1, keepdims=True)
    low_iota = iota((LOW, LOW), 0).astype(F32).astype(BF)

    def place(b, carry):
        fetch(b).wait()
        acc = None
        for c in range(SECTION // LOW):
            cols = pl.ds(c * LOW, LOW)
            code = code_ref[pl.ds(b, 1), cols]
            low = (code & (LOW - 1)).astype(F32).astype(BF)
            high = jnp.broadcast_to(((code // LOW) & (HIGH - 1)).astype(F32).astype(BF), (CAP, LOW))
            flip = (1 - 2 * (code // SECTION)).astype(F32)
            signed = ((dos[b, :, cols].astype(F32) - center) * scale * flip).astype(BF)
            zero = jnp.zeros_like(signed)
            parts = [jnp.where(high == jnp.array(h, BF), signed, zero) for h in range(HIGH)]
            hot = jnp.where(jnp.broadcast_to(low, (LOW, LOW)) == low_iota, jnp.array(1, BF), jnp.array(0, BF))
            part = lax.dot_general(
                jnp.concatenate(parts, axis=0), hot, (((1,), (1,)), ((), ())), preferred_element_type=F32
            )
            acc = part if acc is None else acc + part
        mix[b] = acc
        return carry

    lax.fori_loop(0, blocks, place, 0)

    def cross(i, carry):
        top = pl.multiple_of(i * 8, 8)
        for c in range(LOW // 128):
            cols = pl.ds(c * 128, 128)
            vals = [mix[b, pl.ds(top, 8), cols] for b in range(blocks)]
            step = 1
            while step < blocks:
                nxt = list(vals)
                for b in range(blocks):
                    if not b & step:
                        nxt[b] = vals[b] + vals[b + step]
                        nxt[b + step] = vals[b] - vals[b + step]
                vals = nxt
                step *= 2
            for b in range(blocks):
                mix[b, pl.ds(top, 8), cols] = vals[b]
        return carry

    lax.fori_loop(0, HIGH * CAP // 8, cross, 0)

    lane = iota((16, 128), 1) // 32
    norm = 1.0 / math.sqrt(SECTION * blocks * 4)

    def sample(d, carry):
        row = rows_ref[pl.ds(d, 1), :] & (SECTION - 1)
        table = parity_sign(jnp.broadcast_to(row & (LOW - 1), (LOW, 128)) & iota((LOW, 128), 0)).astype(BF)
        raw = jnp.dot(mix[d].astype(BF), table, preferred_element_type=F32)
        top = row // LOW
        s1 = (1 - 2 * (top & 1)).astype(F32)
        s2 = (1 - 2 * (top // 2)).astype(F32)
        w = (raw[0:CAP] + s1 * raw[CAP : 2 * CAP]) + s2 * (raw[2 * CAP : 3 * CAP] + s1 * raw[3 * CAP :])
        w = w * norm
        for g in range(4):
            out = None
            for q in range(4):
                piece = w[16 * q : 16 * q + 16]
                if q != g:
                    piece = pltpu.roll(piece, 32 * ((q - g) % 4), 1)
                out = piece if out is None else jnp.where(lane == q, piece, out)
            out_ref[g, d] = out.astype(BF)
        return carry

    lax.fori_loop(0, blocks, sample, 0)


def finish_kernel(place_ref, got_ref, proj_ref, out_ref):
    files = got_ref.shape[1]
    group = place_ref[0]
    odd1 = (1 - 2 * (group % 2)).astype(F32)
    odd2 = (1 - 2 * (group // 2)).astype(F32)
    g = [got_ref[i].astype(F32) for i in range(4)]
    total = (g[0] + odd1 * g[1]) + odd2 * (g[2] + odd1 * g[3])
    total = total.reshape(files * 16, 128).astype(BF)
    out = None
    for q in range(4):
        full = lax.dot_general(total, proj_ref[q], (((0,), (0,)), ((), ())), preferred_element_type=F32)
        part = full[32 * q : 32 * q + 32]
        out = part if out is None else out + part
    out_ref[...] = out


def vmem(n):
    return [pl.BlockSpec(memory_space=pltpu.VMEM)] * n


def smem():
    return pl.BlockSpec(memory_space=pltpu.SMEM)


def on_device(
    dosage, variant_slot, center, variant_scale, sample_signs, sample_perm, sample_rows, projection
):
    groups, devs = lax.axis_size("grp"), lax.axis_size("dev")
    both = ("grp", "dev")
    group, dev = lax.axis_index("grp"), lax.axis_index("dev")
    code = pl.pallas_call(
        invert_kernel,
        out_shape=jax.ShapeDtypeStruct((1, SECTION), jnp.int32),
        in_specs=vmem(2),
        out_specs=pl.BlockSpec(memory_space=pltpu.VMEM),
    )(sample_perm[None], sample_signs[None])
    slot_proj = pl.pallas_call(
        slot_kernel,
        out_shape=jax.ShapeDtypeStruct((4, 512, K), BF),
        in_specs=vmem(2),
        out_specs=pl.BlockSpec(memory_space=pltpu.VMEM),
    )(variant_slot[None], projection)
    send = jnp.concatenate([code, sample_rows[None]], axis=1)
    send = jnp.broadcast_to(send, (groups * devs, SECTION + 32))
    got = lax.all_to_all(send, both, 0, 0, tiled=True)
    codes = lax.dynamic_slice(got, (group * devs, 0), (devs, SECTION))
    rows = got[:, SECTION:].reshape(groups, devs, 32).transpose(1, 0, 2).reshape(devs, groups * 32)
    mixed = pl.pallas_call(
        mix_kernel,
        out_shape=jax.ShapeDtypeStruct((groups, devs, 16, 128), BF),
        in_specs=[smem(), pl.BlockSpec(memory_space=pl.ANY)] + vmem(5),
        out_specs=pl.BlockSpec(memory_space=pltpu.VMEM),
        scratch_shapes=[
            pltpu.VMEM((devs, CAP, SECTION), BF),
            pltpu.VMEM((devs, HIGH * CAP, LOW), F32),
            pltpu.SemaphoreType.DMA((devs,)),
        ],
    )(dev[None], dosage, codes, rows, variant_slot[None], center[None], variant_scale[None])
    mixed = mixed.reshape(groups * devs, 16, 128)
    got = lax.all_to_all(mixed, both, 0, 0, tiled=True).reshape(groups, devs, 16, 128)
    return pl.pallas_call(
        finish_kernel,
        out_shape=jax.ShapeDtypeStruct((32, K), F32),
        in_specs=[smem()] + vmem(2),
        out_specs=pl.BlockSpec(memory_space=pltpu.VMEM),
    )(group[None], got, slot_proj)


def solution(mesh):
    return jax.shard_map(
        on_device,
        mesh=mesh,
        in_specs=(
            P("dev", "grp"),
            P(),
            P(),
            P(),
            P(("grp", "dev")),
            P(("grp", "dev")),
            P(("grp", "dev")),
            P(),
        ),
        out_specs=P(("grp", "dev"), None),
        check_vma=False,
    )
```

```python
import math

import jax
import jax.numpy as jnp
from jax import lax
from jax.experimental import pallas as pl
from jax.experimental.pallas import tpu as pltpu
from jax.sharding import PartitionSpec as P

V = 1024
K = 256
SECTION = 1024
LOW = 128
HIGH = SECTION // LOW
CAP = 64
LANES = 128
UNROLL1, UNROLL2, UNROLL3 = 4, 1, 4
BF = jnp.bfloat16
F32 = jnp.float32
NT = (((1,), (1,)), ((), ()))
TN = (((0,), (0,)), ((), ()))


def iota(shape, axis):
    return lax.broadcasted_iota(jnp.int32, shape, axis)


def small(ints):
    return ints.astype(F32).astype(BF)


def invert_kernel(place_ref, perm_ref, sign_ref, rows_ref, out_ref):
    spot = perm_ref[...] & (SECTION - 1)
    row = iota((2 * HIGH, SECTION), 0)
    position = iota((2 * HIGH, SECTION), 1)
    digit = jnp.where(row < HIGH, position % LOW, position // LOW + HIGH * (sign_ref[...] < 0).astype(jnp.int32))
    digit = jnp.where(spot // LOW == row % HIGH, digit, 0)
    hot = jnp.where(small(spot % LOW) == small(iota((LOW, SECTION), 0)), jnp.array(1, BF), jnp.array(0, BF))
    found = lax.dot_general(small(digit), hot, NT, preferred_element_type=F32).astype(jnp.int32)
    code = found[:HIGH] + LOW * found[HIGH:]
    lane = iota((1, LANES), 1)
    mine = jnp.where(lane // 32 == place_ref[0], rows_ref[...] & (SECTION - 1), 0)
    count = out_ref.shape[0]
    for h in range(HIGH):
        out_ref[:, :, h * LANES : (h + 1) * LANES] = jnp.broadcast_to(code[h : h + 1][None], (count, 1, LANES))
    out_ref[:, :, SECTION:] = jnp.broadcast_to(mine[None], (count, 1, LANES))


def ready_kernel(place_ref, dos_ref, slot_ref, cen_ref, scl_ref, proj_ref, out_ref, gain_ref, had_ref, sp_ref, cen_col):
    step = pl.program_id(0)

    @pl.when(step == 0)
    def _():
        mine = jnp.broadcast_to(slot_ref[...], (CAP, V)) == iota((CAP, V), 0) + place_ref[0] * CAP
        center = jnp.sum(jnp.where(mine, jnp.broadcast_to(cen_ref[...], (CAP, V)), 0.0), axis=1, keepdims=True)
        scale = jnp.sum(jnp.where(mine, jnp.broadcast_to(scl_ref[...], (CAP, V)), 0.0), axis=1, keepdims=True)
        cen_col[...] = jnp.broadcast_to(center, (CAP, LANES))
        gain_ref[...] = jnp.broadcast_to(scale, (CAP, LANES))
        bits = iota((LOW, LOW), 0) & iota((LOW, LOW), 1)
        bits = bits ^ (bits >> 4)
        bits = bits ^ (bits >> 2)
        bits = bits ^ (bits >> 1)
        had_ref[...] = small(1 - 2 * (bits & 1))

    center = cen_col[:, 0:1]
    for i in range(out_ref.shape[0]):
        out_ref[i] = (dos_ref[:, i * SECTION : (i + 1) * SECTION].astype(F32) - center).astype(BF)

    rows = sp_ref.shape[0]
    slot = slot_ref[...]
    target = (slot // 16 % 4) * 512 + slot // CAP * 16 + slot % 16
    hot = (jnp.broadcast_to(target, (rows, V)) == iota((rows, V), 0) + step * rows).astype(F32).astype(BF)
    sp_ref[...] = jnp.dot(hot, proj_ref[...], preferred_element_type=F32).astype(BF)


def mix_kernel(place_ref, xs_ref, got_ref, gain_ref, had_ref, out_ref, mix, tables):
    blocks = xs_ref.shape[0]
    group = place_ref[0]
    norm = 1.0 / math.sqrt(SECTION * blocks * 4)
    one, zero = jnp.array(1, BF), jnp.array(0, BF)

    def place(b, carry):
        code = got_ref[group * blocks + b, :, 0:SECTION]
        low = jnp.broadcast_to(small(code & (LOW - 1)), (LOW, SECTION))
        flip = jnp.broadcast_to(small(1 - 2 * (code // SECTION)), (LOW, SECTION))
        high = jnp.broadcast_to(small((code // LOW) & (HIGH - 1)), (CAP, SECTION))
        shifted = xs_ref[b]
        parts = [jnp.where(high == jnp.array(h, BF), shifted, zero) for h in range(HIGH)]
        hot = jnp.where(low == small(iota((LOW, SECTION), 0)), flip, zero)
        spot = lax.dot_general(jnp.concatenate(parts, axis=0), hot, NT, preferred_element_type=F32).astype(BF)
        mix[b] = spot.reshape(mix.shape[1:])
        row = sum(got_ref[g * blocks + b, :, SECTION:] for g in range(4))
        hot = jnp.where(jnp.broadcast_to(small(row & (LOW - 1)), (LOW, LANES)) == small(iota((LOW, LANES), 0)), one, zero)
        tables[b] = jnp.dot(had_ref[...], hot, preferred_element_type=F32).astype(BF)
        return carry

    lax.fori_loop(0, blocks, place, 0, unroll=UNROLL1)

    def cross(i, carry):
        vals = [mix[b, i] for b in range(blocks)]
        step = 1
        while step < blocks:
            nxt = list(vals)
            for b in range(blocks):
                if not b & step:
                    nxt[b] = vals[b] + vals[b + step]
                    nxt[b + step] = vals[b] - vals[b + step]
            vals = nxt
            step *= 2
        for b in range(blocks):
            mix[b, i] = vals[b]
        return carry

    lax.fori_loop(0, mix.shape[1], cross, 0, unroll=UNROLL2)

    lane = iota((16, LANES), 1) // 32
    gain = gain_ref[...] * norm

    def sample(d, carry):
        raw = jnp.dot(mix[d].reshape(HIGH * CAP, LOW), tables[d], preferred_element_type=F32)
        parts = [raw[h * CAP : (h + 1) * CAP] for h in range(HIGH)]
        top = sum(got_ref[g * blocks + d, :, SECTION:] for g in range(4)) // LOW
        while len(parts) > 1:
            sign = (1 - 2 * (top & 1)).astype(F32)
            parts = [parts[i] + sign * parts[i + 1] for i in range(0, len(parts), 2)]
            top = top // 2
        w = parts[0] * gain
        spun = [w[16 * q : 16 * q + 16] for q in range(4)]
        spun = [spun[0]] + [pltpu.roll(spun[q], 32 * q, 1) for q in range(1, 4)]
        for g in range(4):
            out = spun[0]
            for q in range(1, 4):
                out = jnp.where(lane == (g + q) % 4, spun[q], out)
            out_ref[g, d] = out.astype(BF)
        return carry

    lax.fori_loop(0, blocks, sample, 0, unroll=UNROLL3)


def finish_kernel(place_ref, got_ref, proj_ref, out_ref):
    files = got_ref.shape[1]
    group = place_ref[0]
    odd1 = (1 - 2 * (group % 2)).astype(F32)
    odd2 = (1 - 2 * (group // 2)).astype(F32)
    g = [got_ref[i].astype(F32) for i in range(4)]
    total = (g[0] + odd1 * g[1]) + odd2 * (g[2] + odd1 * g[3])
    total = total.reshape(files * 16, 128).astype(BF)
    out = None
    for q in range(4):
        full = lax.dot_general(total, proj_ref[(q + 4 - group) % 4], TN, preferred_element_type=F32)
        part = full[32 * q : 32 * q + 32]
        out = part if out is None else out + part
    out_ref[...] = out


def vmem(n):
    return [pl.BlockSpec(memory_space=pltpu.VMEM)] * n


def limit(mib):
    return pltpu.CompilerParams(vmem_limit_bytes=mib << 20)


def smem():
    return pl.BlockSpec(memory_space=pltpu.SMEM)


def on_device(
    dosage, variant_slot, center, variant_scale, sample_signs, sample_perm, sample_rows, projection
):
    groups, devs = lax.axis_size("grp"), lax.axis_size("dev")
    both = ("grp", "dev")
    group, dev = lax.axis_index("grp"), lax.axis_index("dev")
    send = pl.pallas_call(
        invert_kernel,
        out_shape=jax.ShapeDtypeStruct((groups * devs, 1, SECTION + LANES), jnp.int32),
        in_specs=[smem()] + vmem(3),
        out_specs=pl.BlockSpec(memory_space=pltpu.VMEM),
        compiler_params=limit(8),
    )(group[None], sample_perm[None], sample_signs[None], jnp.tile(sample_rows, 4)[None])
    steps = 8
    per = devs // steps
    xs, gain, had, slot_proj = pl.pallas_call(
        ready_kernel,
        grid=(steps,),
        out_shape=(
            jax.ShapeDtypeStruct((devs, CAP, SECTION), BF),
            jax.ShapeDtypeStruct((CAP, LANES), F32),
            jax.ShapeDtypeStruct((LOW, LOW), BF),
            jax.ShapeDtypeStruct((devs * CAP, K), BF),
        ),
        in_specs=[
            smem(),
            pl.BlockSpec((CAP, per * SECTION), lambda i: (0, i)),
            pl.BlockSpec((1, V), lambda i: (0, 0)),
            pl.BlockSpec((1, V), lambda i: (0, 0)),
            pl.BlockSpec((1, V), lambda i: (0, 0)),
            pl.BlockSpec((V, K), lambda i: (0, 0)),
        ],
        out_specs=(
            pl.BlockSpec((per, CAP, SECTION), lambda i: (i, 0, 0)),
            pl.BlockSpec((CAP, LANES), lambda i: (0, 0)),
            pl.BlockSpec((LOW, LOW), lambda i: (0, 0)),
            pl.BlockSpec((devs * CAP // steps, K), lambda i: (i, 0)),
        ),
        scratch_shapes=[pltpu.VMEM((CAP, LANES), F32)],
        compiler_params=limit(12),
    )(dev[None], dosage, variant_slot[None], center[None], variant_scale[None], projection)
    got = lax.all_to_all(send, both, 0, 0, tiled=True)
    mixed = pl.pallas_call(
        mix_kernel,
        out_shape=jax.ShapeDtypeStruct((groups, devs, 16, LANES), BF),
        in_specs=[smem()] + vmem(4),
        out_specs=pl.BlockSpec(memory_space=pltpu.VMEM),
        compiler_params=limit(24),
        scratch_shapes=[
            pltpu.VMEM((devs, HIGH * CAP // 16, 16, LOW), BF),
            pltpu.VMEM((devs, LOW, LANES), BF),
        ],
    )(group[None], xs, got, gain, had)
    mixed = mixed.reshape(groups * devs, 16, 128)
    got = lax.all_to_all(mixed, both, 0, 0, tiled=True).reshape(groups, devs, 16, 128)
    return pl.pallas_call(
        finish_kernel,
        out_shape=jax.ShapeDtypeStruct((32, K), F32),
        in_specs=[smem()] + vmem(2),
        out_specs=pl.BlockSpec(memory_space=pltpu.VMEM),
        compiler_params=limit(8),
    )(group[None], got, slot_proj.reshape(4, devs * 16, K))


def solution(mesh):
    return jax.shard_map(
        on_device,
        mesh=mesh,
        in_specs=(
            P("dev", "grp"),
            P(),
            P(),
            P(),
            P(("grp", "dev")),
            P(("grp", "dev")),
            P(("grp", "dev")),
            P(),
        ),
        out_specs=P(("grp", "dev"), None),
        check_vma=False,
    )
```

```python
import math

import jax
import jax.numpy as jnp
from jax import lax
from jax.experimental import pallas as pl
from jax.experimental.pallas import tpu as pltpu
from jax.sharding import PartitionSpec as P

V = 1024
K = 256
SECTION = 1024
LOW = 256
HIGH = SECTION // LOW
CAP = 64
LANES = 128
UNROLL1, UNROLL2, UNROLL3, UNROLL4 = 8, 1, 8, 8
BF = jnp.bfloat16
F32 = jnp.float32
NT = (((1,), (1,)), ((), ()))
TN = (((0,), (0,)), ((), ()))


def iota(shape, axis):
    return lax.broadcasted_iota(jnp.int32, shape, axis)


def small(ints):
    return ints.astype(F32).astype(BF)


def copy_in(pairs, sem):
    copies = [pltpu.make_async_copy(src, dst, sem.at[i]) for i, (src, dst) in enumerate(pairs)]
    for c in copies:
        c.start()
    return copies


def invert_kernel(place_ref, perm_hbm, sign_hbm, rows_hbm, out_hbm, perm_ref, sign_ref, rows_ref, send_ref, sem):
    for c in copy_in(((perm_hbm, perm_ref), (sign_hbm, sign_ref), (rows_hbm, rows_ref)), sem):
        c.wait()
    spot = perm_ref[...] & (SECTION - 1)
    group_of = SECTION // LANES
    row = iota((2 * group_of, SECTION), 0)
    position = iota((2 * group_of, SECTION), 1)
    negative = (sign_ref[...] < 0).astype(jnp.int32)
    digit = jnp.where(row < group_of, position % LANES, position // LANES + group_of * negative)
    digit = jnp.where(spot // LANES == row % group_of, digit, 0)
    hot = jnp.where(small(spot % LANES) == small(iota((LANES, SECTION), 0)), jnp.array(1, BF), jnp.array(0, BF))
    found = lax.dot_general(small(digit), hot, NT, preferred_element_type=F32).astype(jnp.int32)
    code = found[:group_of] + LANES * found[group_of:]
    rows = jnp.concatenate([rows_ref[...] & (SECTION - 1)] * 4, axis=1)
    mine = jnp.where(iota((1, LANES), 1) // 32 == place_ref[0], rows, 0)
    count = send_ref.shape[0]
    for h in range(group_of):
        send_ref[:, :, h * LANES : (h + 1) * LANES] = jnp.broadcast_to(code[h : h + 1][None], (count, 1, LANES))
    send_ref[:, :, SECTION:] = jnp.broadcast_to(mine[None], (count, 1, LANES))
    total = out_hbm.shape[0] // count
    copies = copy_in([(send_ref, out_hbm.at[pl.ds(i * count, count)]) for i in range(total)], sem)
    for c in copies:
        c.wait()


def ready_kernel(
    place_ref, dos_hbm, slot_hbm, cen_hbm, scl_hbm, proj_hbm, out_hbm, gain_ref, had_ref, sp_ref,
    dos, xs, slot_ref, cen_ref, scl_ref, proj_ref, sem,
):
    chunks = dos.shape[0]
    per = xs.shape[1]
    width = per * SECTION
    pairs = [(slot_hbm, slot_ref), (cen_hbm, cen_ref), (scl_hbm, scl_ref)]
    pairs += [(dos_hbm.at[:, pl.ds(c * width, width)], dos.at[c]) for c in range(chunks)]
    copies = copy_in(pairs + [(proj_hbm, proj_ref)], sem)
    bits = iota((LOW, LOW), 0) & iota((LOW, LOW), 1)
    bits = bits ^ (bits >> 4)
    bits = bits ^ (bits >> 2)
    bits = bits ^ (bits >> 1)
    had_ref[...] = small(1 - 2 * (bits & 1))
    for c in copies[:3]:
        c.wait()
    mine = jnp.broadcast_to(slot_ref[...], (CAP, V)) == iota((CAP, V), 0) + place_ref[0] * CAP
    center = jnp.sum(jnp.where(mine, jnp.broadcast_to(cen_ref[...], (CAP, V)), 0.0), axis=1, keepdims=True)
    scale = jnp.sum(jnp.where(mine, jnp.broadcast_to(scl_ref[...], (CAP, V)), 0.0), axis=1, keepdims=True)
    gain_ref[...] = jnp.broadcast_to(scale, (CAP, LANES))
    sends = []
    for c in range(chunks):
        copies[3 + c].wait()
        for i in range(per):
            xs[c, i] = (dos[c, :, i * SECTION : (i + 1) * SECTION].astype(F32) - center).astype(BF)
        sends.append(pltpu.make_async_copy(xs.at[c], out_hbm.at[pl.ds(c * per, per)], sem.at[c]))
        sends[-1].start()
    copies[-1].wait()

    slot = slot_ref[...]
    target = (slot // 16 % 4) * 512 + slot // CAP * 16 + slot % 16
    rows = 256
    for c in range(sp_ref.shape[0] // rows):
        hot = (jnp.broadcast_to(target, (rows, V)) == iota((rows, V), 0) + c * rows).astype(F32).astype(BF)
        sp_ref[c * rows : (c + 1) * rows] = jnp.dot(hot, proj_ref[...], preferred_element_type=F32).astype(BF)
    for c in sends:
        c.wait()


def mix_kernel(place_ref, xs_hbm, got_ref, gain_ref, had_ref, out_ref, xs_ref, spots, mix, tables, sem):
    blocks = xs_ref.shape[0]
    group = place_ref[0]

    def fetch(b):
        return pltpu.make_async_copy(xs_hbm.at[b], xs_ref.at[b], sem.at[b])

    for b in range(blocks):
        fetch(b).start()
    norm = 1.0 / math.sqrt(SECTION * blocks * 4)
    one, zero = jnp.array(1, BF), jnp.array(0, BF)

    def table(i, carry):
        row = jnp.concatenate([sum(got_ref[g * blocks + 2 * i + u, :, SECTION:] for g in range(4)) for u in range(2)], axis=1)
        hot = jnp.where(jnp.broadcast_to(small(row & (LOW - 1)), (LOW, 2 * LANES)) == small(iota((LOW, 2 * LANES), 0)), one, zero)
        both = jnp.dot(had_ref[...], hot, preferred_element_type=F32).astype(BF)
        tables[2 * i] = both[:, :LANES]
        tables[2 * i + 1] = both[:, LANES:]
        return carry

    lax.fori_loop(0, blocks // 2, table, 0, unroll=UNROLL4)

    def place(i, carry):
        for u in range(UNROLL1):
            fetch(i * UNROLL1 + u).wait()
        for u in range(UNROLL1):
            b = i * UNROLL1 + u
            code = got_ref[group * blocks + b, :, 0:SECTION]
            low = jnp.broadcast_to(small(code & (LOW - 1)), (LOW, SECTION))
            flip = jnp.broadcast_to(small(1 - 2 * (code // SECTION)), (LOW, SECTION))
            high = jnp.broadcast_to(small((code // LOW) & (HIGH - 1)), (CAP, SECTION))
            shifted = xs_ref[b]
            parts = [jnp.where(high == jnp.array(h, BF), shifted, zero) for h in range(HIGH)]
            hot = jnp.where(low == small(iota((LOW, SECTION), 0)), flip, zero)
            spot = lax.dot_general(jnp.concatenate(parts, axis=0), hot, NT, preferred_element_type=F32)
            spots[b] = spot.reshape(spots.shape[1:])
        return carry

    lax.fori_loop(0, blocks // UNROLL1, place, 0)

    def cross(i, carry):
        cols = pl.ds(pl.multiple_of(i % (LOW // LANES) * LANES, LANES), LANES)
        i = i // (LOW // LANES)
        vals = [spots[b, i, :, cols].astype(BF) for b in range(blocks)]
        step = 1
        while step < blocks:
            nxt = list(vals)
            for b in range(blocks):
                if not b & step:
                    nxt[b] = vals[b] + vals[b + step]
                    nxt[b + step] = vals[b] - vals[b + step]
            vals = nxt
            step *= 2
        for b in range(blocks):
            mix[b, i, :, cols] = vals[b]
        return carry

    lax.fori_loop(0, mix.shape[1] * (LOW // LANES), cross, 0, unroll=UNROLL2)

    lane = iota((16, LANES), 1) // 32
    gain = gain_ref[...] * norm

    def sample(d, carry):
        raw = jnp.dot(mix[d].reshape(HIGH * CAP, LOW), tables[d], preferred_element_type=F32)
        parts = [raw[h * CAP : (h + 1) * CAP] for h in range(HIGH)]
        top = sum(got_ref[g * blocks + d, :, SECTION:] for g in range(4)) // LOW
        while len(parts) > 1:
            sign = (1 - 2 * (top & 1)).astype(F32)
            parts = [parts[i] + sign * parts[i + 1] for i in range(0, len(parts), 2)]
            top = top // 2
        w = parts[0] * gain
        spun = [w[16 * q : 16 * q + 16] for q in range(4)]
        spun = [spun[0]] + [pltpu.roll(spun[q], 32 * q, 1) for q in range(1, 4)]
        for g in range(4):
            out = spun[0]
            for q in range(1, 4):
                out = jnp.where(lane == (g + q) % 4, spun[q], out)
            out_ref[g, d] = out.astype(BF)
        return carry

    lax.fori_loop(0, blocks, sample, 0, unroll=UNROLL3)


def finish_kernel(place_ref, got_ref, proj_ref, out_ref):
    files = got_ref.shape[1]
    group = place_ref[0]
    odd1 = (1 - 2 * (group % 2)).astype(F32)
    odd2 = (1 - 2 * (group // 2)).astype(F32)
    g = [got_ref[i].astype(F32) for i in range(4)]
    total = (g[0] + odd1 * g[1]) + odd2 * (g[2] + odd1 * g[3])
    total = total.reshape(files * 16, 128).astype(BF)
    out = None
    for q in range(4):
        full = lax.dot_general(total, proj_ref[(q + 4 - group) % 4], TN, preferred_element_type=F32)
        part = full[32 * q : 32 * q + 32]
        out = part if out is None else out + part
    out_ref[...] = out


def vmem(n):
    return [pl.BlockSpec(memory_space=pltpu.VMEM)] * n


def limit(mib):
    return pltpu.CompilerParams(vmem_limit_bytes=mib << 20)


def hbm(n):
    return [pl.BlockSpec(memory_space=pltpu.HBM)] * n


def stay(*arrays):
    return [pltpu.with_memory_space_constraint(a, pltpu.HBM) for a in arrays]


def smem():
    return pl.BlockSpec(memory_space=pltpu.SMEM)


def on_device(
    dosage, variant_slot, center, variant_scale, sample_signs, sample_perm, sample_rows, projection
):
    groups, devs = lax.axis_size("grp"), lax.axis_size("dev")
    both = ("grp", "dev")
    group, dev = lax.axis_index("grp"), lax.axis_index("dev")
    send = pl.pallas_call(
        invert_kernel,
        out_shape=jax.ShapeDtypeStruct((groups * devs, 1, SECTION + LANES), jnp.int32),
        in_specs=[smem()] + hbm(3),
        out_specs=hbm(1)[0],
        scratch_shapes=[
            pltpu.VMEM((1, SECTION), jnp.int32),
            pltpu.VMEM((1, SECTION), jnp.int32),
            pltpu.VMEM((1, 32), jnp.int32),
            pltpu.VMEM((8, 1, SECTION + LANES), jnp.int32),
            pltpu.SemaphoreType.DMA((groups * devs // 8,)),
        ],
        compiler_params=limit(8),
    )(group[None], *stay(sample_perm[None], sample_signs[None], sample_rows[None]))
    chunks = 8
    per = devs // chunks
    xs, gain, had, slot_proj = pl.pallas_call(
        ready_kernel,
        out_shape=(
            pltpu.HBM((devs, CAP, SECTION), BF),
            jax.ShapeDtypeStruct((CAP, LANES), F32),
            jax.ShapeDtypeStruct((LOW, LOW), BF),
            jax.ShapeDtypeStruct((devs * CAP, K), BF),
        ),
        in_specs=[smem()] + hbm(5),
        out_specs=tuple(hbm(1) + vmem(3)),
        scratch_shapes=[
            pltpu.VMEM((chunks, CAP, per * SECTION), BF),
            pltpu.VMEM((chunks, per, CAP, SECTION), BF),
            pltpu.VMEM((1, V), jnp.int32),
            pltpu.VMEM((1, V), F32),
            pltpu.VMEM((1, V), F32),
            pltpu.VMEM((V, K), BF),
            pltpu.SemaphoreType.DMA((chunks + 4,)),
        ],
        compiler_params=limit(16),
    )(dev[None], *stay(dosage, variant_slot[None], center[None], variant_scale[None], projection))
    got = lax.all_to_all(send, both, 0, 0, tiled=True)
    mixed = pl.pallas_call(
        mix_kernel,
        out_shape=jax.ShapeDtypeStruct((groups, devs, 16, LANES), BF),
        in_specs=[smem()] + hbm(1) + vmem(3),
        out_specs=pl.BlockSpec(memory_space=pltpu.VMEM),
        compiler_params=limit(32),
        scratch_shapes=[
            pltpu.VMEM((devs, CAP, SECTION), BF),
            pltpu.VMEM((devs, HIGH * CAP // 16, 16, LOW), F32),
            pltpu.VMEM((devs, HIGH * CAP // 16, 16, LOW), BF),
            pltpu.VMEM((devs, LOW, LANES), BF),
            pltpu.SemaphoreType.DMA((devs,)),
        ],
    )(group[None], *stay(xs), got, gain, had)
    mixed = mixed.reshape(groups * devs, 16, 128)
    got = lax.all_to_all(mixed, both, 0, 0, tiled=True).reshape(groups, devs, 16, 128)
    return pl.pallas_call(
        finish_kernel,
        out_shape=jax.ShapeDtypeStruct((32, K), F32),
        in_specs=[smem()] + vmem(2),
        out_specs=pl.BlockSpec(memory_space=pltpu.VMEM),
        compiler_params=limit(8),
    )(group[None], got, slot_proj.reshape(4, devs * 16, K))


def solution(mesh):
    return jax.shard_map(
        on_device,
        mesh=mesh,
        in_specs=(
            P("dev", "grp"),
            P(),
            P(),
            P(),
            P(("grp", "dev")),
            P(("grp", "dev")),
            P(("grp", "dev")),
            P(),
        ),
        out_specs=P(("grp", "dev"), None),
        check_vma=False,
    )
```

```python
import math

import jax
import jax.numpy as jnp
from jax import lax
from jax.experimental import pallas as pl
from jax.experimental.pallas import tpu as pltpu
from jax.sharding import PartitionSpec as P

V = 1024
K = 256
SECTION = 1024
LOW = 256
HIGH = SECTION // LOW
CAP = 64
LANES = 128
UNROLL1, UNROLL2, UNROLL3, UNROLL4, FUSED = 16, 64, 16, 8, 4
BF = jnp.bfloat16
F32 = jnp.float32
NT = (((1,), (1,)), ((), ()))
TN = (((0,), (0,)), ((), ()))


def iota(shape, axis):
    return lax.broadcasted_iota(jnp.int32, shape, axis)


def small(ints):
    return ints.astype(F32).astype(BF)


def copy_in(pairs, sem):
    copies = [pltpu.make_async_copy(src, dst, sem.at[i]) for i, (src, dst) in enumerate(pairs)]
    for c in copies:
        c.start()
    return copies


def invert_kernel(place_ref, perm_hbm, sign_hbm, rows_hbm, out_hbm, perm_ref, sign_ref, rows_ref, send_ref, sem):
    for c in copy_in(((perm_hbm, perm_ref), (sign_hbm, sign_ref), (rows_hbm, rows_ref)), sem):
        c.wait()
    spot = perm_ref[...] & (SECTION - 1)
    group_of = SECTION // LANES
    row = iota((2 * group_of, SECTION), 0)
    position = iota((2 * group_of, SECTION), 1)
    negative = (sign_ref[...] < 0).astype(jnp.int32)
    digit = jnp.where(row < group_of, position % LANES, position // LANES + group_of * negative)
    digit = jnp.where(spot // LANES == row % group_of, digit, 0)
    hot = jnp.where(small(spot % LANES) == small(iota((LANES, SECTION), 0)), jnp.array(1, BF), jnp.array(0, BF))
    found = lax.dot_general(small(digit), hot, NT, preferred_element_type=F32).astype(jnp.int32)
    code = found[:group_of] + LANES * found[group_of:]
    rows = jnp.concatenate([rows_ref[...] & (SECTION - 1)] * 4, axis=1)
    mine = jnp.where(iota((1, LANES), 1) // 32 == place_ref[0], rows, 0)
    count = send_ref.shape[0]
    for h in range(group_of):
        send_ref[:, :, h * LANES : (h + 1) * LANES] = jnp.broadcast_to(code[h : h + 1][None], (count, 1, LANES))
    send_ref[:, :, SECTION:] = jnp.broadcast_to(mine[None], (count, 1, LANES))
    total = out_hbm.shape[0] // count
    copies = copy_in([(send_ref, out_hbm.at[pl.ds(i * count, count)]) for i in range(total)], sem)
    for c in copies:
        c.wait()


def ready_kernel(
    place_ref, dos_hbm, slot_hbm, cen_hbm, scl_hbm, proj_hbm, out_hbm, gain_ref, had_ref, sp_ref,
    dos, xs, slot_ref, cen_ref, scl_ref, proj_ref, sem,
):
    chunks = dos.shape[0]
    per = xs.shape[1]
    width = per * SECTION
    pairs = [(slot_hbm, slot_ref), (cen_hbm, cen_ref), (scl_hbm, scl_ref)]
    pairs += [(dos_hbm.at[:, pl.ds(c * width, width)], dos.at[c]) for c in range(chunks)]
    copies = copy_in(pairs + [(proj_hbm, proj_ref)], sem)
    bits = iota((LOW, LOW), 0) & iota((LOW, LOW), 1)
    bits = bits ^ (bits >> 4)
    bits = bits ^ (bits >> 2)
    bits = bits ^ (bits >> 1)
    had_ref[...] = small(1 - 2 * (bits & 1))
    for c in copies[:3]:
        c.wait()
    mine = jnp.broadcast_to(slot_ref[...], (CAP, V)) == iota((CAP, V), 0) + place_ref[0] * CAP
    center = jnp.sum(jnp.where(mine, jnp.broadcast_to(cen_ref[...], (CAP, V)), 0.0), axis=1, keepdims=True)
    scale = jnp.sum(jnp.where(mine, jnp.broadcast_to(scl_ref[...], (CAP, V)), 0.0), axis=1, keepdims=True)
    gain_ref[...] = jnp.broadcast_to(scale, (CAP, LANES))
    sends = []
    for c in range(chunks):
        copies[3 + c].wait()
        for i in range(per):
            xs[c, i] = (dos[c, :, i * SECTION : (i + 1) * SECTION].astype(F32) - center).astype(BF)
        sends.append(pltpu.make_async_copy(xs.at[c], out_hbm.at[pl.ds(c * per, per)], sem.at[c]))
        sends[-1].start()
    copies[-1].wait()

    slot = slot_ref[...]
    target = (slot // 16 % 4) * 512 + slot // CAP * 16 + slot % 16
    rows = 256
    for c in range(sp_ref.shape[0] // rows):
        hot = (jnp.broadcast_to(target, (rows, V)) == iota((rows, V), 0) + c * rows).astype(F32).astype(BF)
        sp_ref[c * rows : (c + 1) * rows] = jnp.dot(hot, proj_ref[...], preferred_element_type=F32).astype(BF)
    for c in sends:
        c.wait()


def butterflies(vals, step):
    while step < len(vals):
        pairs = {b: (vals[b] + vals[b + step], vals[b] - vals[b + step]) for b in range(len(vals)) if not b & step}
        vals = [pairs[b & ~step][1 if b & step else 0] for b in range(len(vals))]
        step *= 2
    return vals


def mix_kernel(place_ref, xs_hbm, got_ref, gain_ref, had_ref, out_ref, xs_ref, spots, tables, sem):
    blocks = xs_ref.shape[0]
    group = place_ref[0]

    def fetch(b):
        return pltpu.make_async_copy(xs_hbm.at[b], xs_ref.at[b], sem.at[b])

    for b in range(blocks):
        fetch(b).start()
    norm = 1.0 / math.sqrt(SECTION * blocks * 4)
    one, zero = jnp.array(1, BF), jnp.array(0, BF)

    def table(i, carry):
        row = jnp.concatenate([sum(got_ref[g * blocks + 2 * i + u, :, SECTION:] for g in range(4)) for u in range(2)], axis=1)
        hot = jnp.where(jnp.broadcast_to(small(row & (LOW - 1)), (LOW, 2 * LANES)) == small(iota((LOW, 2 * LANES), 0)), one, zero)
        both = jnp.dot(had_ref[...], hot, preferred_element_type=F32).astype(BF)
        tables[2 * i] = both[:, :LANES]
        tables[2 * i + 1] = both[:, LANES:]
        return carry

    lax.fori_loop(0, blocks // 2, table, 0, unroll=UNROLL4)

    def place(i, carry):
        for u in range(UNROLL1):
            fetch(i * UNROLL1 + u).wait()
        held = []
        for u in range(UNROLL1):
            b = i * UNROLL1 + u
            code = got_ref[group * blocks + b, :, 0:SECTION]
            low = jnp.broadcast_to(small(code & (LOW - 1)), (LOW, SECTION))
            flip = jnp.broadcast_to(small(1 - 2 * (code // SECTION)), (LOW, SECTION))
            high = jnp.broadcast_to(small((code // LOW) & (HIGH - 1)), (CAP, SECTION))
            shifted = xs_ref[b]
            parts = [jnp.where(high == jnp.array(h, BF), shifted, zero) for h in range(HIGH)]
            hot = jnp.where(low == small(iota((LOW, SECTION), 0)), flip, zero)
            spot = lax.dot_general(jnp.concatenate(parts, axis=0), hot, NT, preferred_element_type=F32)
            held.append(spot)
            if len(held) == FUSED:
                held = butterflies(held, 1)
                for v in range(FUSED):
                    spots[b - FUSED + 1 + v] = held[v]
                held = []
        return carry

    lax.fori_loop(0, blocks // UNROLL1, place, 0)

    def cross(i, carry):
        rows = pl.ds(pl.multiple_of(i // (LOW // LANES) * 8, 8), 8)
        cols = pl.ds(pl.multiple_of(i % (LOW // LANES) * LANES, LANES), LANES)
        vals = butterflies([spots[b, rows, cols] for b in range(blocks)], FUSED)
        for b in range(blocks):
            spots[b, rows, cols] = vals[b]
        return carry

    lax.fori_loop(0, HIGH * CAP // 8 * (LOW // LANES), cross, 0, unroll=UNROLL2)

    lane = iota((16, LANES), 1) // 32
    gain = gain_ref[...] * norm

    def sample(d, carry):
        raw = jnp.dot(spots[d].astype(BF), tables[d], preferred_element_type=F32)
        parts = [raw[h * CAP : (h + 1) * CAP] for h in range(HIGH)]
        top = sum(got_ref[g * blocks + d, :, SECTION:] for g in range(4)) // LOW
        while len(parts) > 1:
            sign = (1 - 2 * (top & 1)).astype(F32)
            parts = [parts[i] + sign * parts[i + 1] for i in range(0, len(parts), 2)]
            top = top // 2
        w = parts[0] * gain
        spun = [w[16 * q : 16 * q + 16] for q in range(4)]
        spun = [spun[0]] + [pltpu.roll(spun[q], 32 * q, 1) for q in range(1, 4)]
        for g in range(4):
            out = spun[0]
            for q in range(1, 4):
                out = jnp.where(lane == (g + q) % 4, spun[q], out)
            out_ref[g, d] = out.astype(BF)
        return carry

    lax.fori_loop(0, blocks, sample, 0, unroll=UNROLL3)


def finish_kernel(place_ref, got_ref, proj_ref, out_ref):
    files = got_ref.shape[1]
    group = place_ref[0]
    odd1 = (1 - 2 * (group % 2)).astype(F32)
    odd2 = (1 - 2 * (group // 2)).astype(F32)
    g = [got_ref[i].astype(F32) for i in range(4)]
    total = (g[0] + odd1 * g[1]) + odd2 * (g[2] + odd1 * g[3])
    total = total.reshape(files * 16, 128).astype(BF)
    out = None
    for q in range(4):
        full = lax.dot_general(total, proj_ref[(q + 4 - group) % 4], TN, preferred_element_type=F32)
        part = full[32 * q : 32 * q + 32]
        out = part if out is None else out + part
    out_ref[...] = out


def vmem(n):
    return [pl.BlockSpec(memory_space=pltpu.VMEM)] * n


def limit(mib):
    return pltpu.CompilerParams(vmem_limit_bytes=mib << 20)


def hbm(n):
    return [pl.BlockSpec(memory_space=pltpu.HBM)] * n


def stay(*arrays):
    return [pltpu.with_memory_space_constraint(a, pltpu.HBM) for a in arrays]


def smem():
    return pl.BlockSpec(memory_space=pltpu.SMEM)


def on_device(
    dosage, variant_slot, center, variant_scale, sample_signs, sample_perm, sample_rows, projection
):
    groups, devs = lax.axis_size("grp"), lax.axis_size("dev")
    both = ("grp", "dev")
    group, dev = lax.axis_index("grp"), lax.axis_index("dev")
    send = pl.pallas_call(
        invert_kernel,
        out_shape=jax.ShapeDtypeStruct((groups * devs, 1, SECTION + LANES), jnp.int32),
        in_specs=[smem()] + hbm(3),
        out_specs=hbm(1)[0],
        scratch_shapes=[
            pltpu.VMEM((1, SECTION), jnp.int32),
            pltpu.VMEM((1, SECTION), jnp.int32),
            pltpu.VMEM((1, 32), jnp.int32),
            pltpu.VMEM((8, 1, SECTION + LANES), jnp.int32),
            pltpu.SemaphoreType.DMA((groups * devs // 8,)),
        ],
        compiler_params=limit(8),
    )(group[None], *stay(sample_perm[None], sample_signs[None], sample_rows[None]))
    chunks = 8
    per = devs // chunks
    xs, gain, had, slot_proj = pl.pallas_call(
        ready_kernel,
        out_shape=(
            pltpu.HBM((devs, CAP, SECTION), BF),
            jax.ShapeDtypeStruct((CAP, LANES), F32),
            jax.ShapeDtypeStruct((LOW, LOW), BF),
            jax.ShapeDtypeStruct((devs * CAP, K), BF),
        ),
        in_specs=[smem()] + hbm(5),
        out_specs=tuple(hbm(1) + vmem(3)),
        scratch_shapes=[
            pltpu.VMEM((chunks, CAP, per * SECTION), BF),
            pltpu.VMEM((chunks, per, CAP, SECTION), BF),
            pltpu.VMEM((1, V), jnp.int32),
            pltpu.VMEM((1, V), F32),
            pltpu.VMEM((1, V), F32),
            pltpu.VMEM((V, K), BF),
            pltpu.SemaphoreType.DMA((chunks + 4,)),
        ],
        compiler_params=limit(16),
    )(dev[None], *stay(dosage, variant_slot[None], center[None], variant_scale[None], projection))
    got = lax.all_to_all(send, both, 0, 0, tiled=True)
    mixed = pl.pallas_call(
        mix_kernel,
        out_shape=jax.ShapeDtypeStruct((groups, devs, 16, LANES), BF),
        in_specs=[smem()] + hbm(1) + vmem(3),
        out_specs=pl.BlockSpec(memory_space=pltpu.VMEM),
        compiler_params=limit(32),
        scratch_shapes=[
            pltpu.VMEM((devs, CAP, SECTION), BF),
            pltpu.VMEM((devs, HIGH * CAP, LOW), F32),
            pltpu.VMEM((devs, LOW, LANES), BF),
            pltpu.SemaphoreType.DMA((devs,)),
        ],
    )(group[None], *stay(xs), got, gain, had)
    mixed = mixed.reshape(groups * devs, 16, 128)
    got = lax.all_to_all(mixed, both, 0, 0, tiled=True).reshape(groups, devs, 16, 128)
    return pl.pallas_call(
        finish_kernel,
        out_shape=jax.ShapeDtypeStruct((32, K), F32),
        in_specs=[smem()] + vmem(2),
        out_specs=pl.BlockSpec(memory_space=pltpu.VMEM),
        compiler_params=limit(8),
    )(group[None], got, slot_proj.reshape(4, devs * 16, K))


def solution(mesh):
    return jax.shard_map(
        on_device,
        mesh=mesh,
        in_specs=(
            P("dev", "grp"),
            P(),
            P(),
            P(),
            P(("grp", "dev")),
            P(("grp", "dev")),
            P(("grp", "dev")),
            P(),
        ),
        out_specs=P(("grp", "dev"), None),
        check_vma=False,
    )
```

```python
import math

import jax
import jax.numpy as jnp
from jax import lax
from jax.experimental import pallas as pl
from jax.experimental.pallas import tpu as pltpu
from jax.sharding import PartitionSpec as P

V = 1024
K = 256
SECTION = 1024
LOW = 256
HIGH = SECTION // LOW
CAP = 64
LANES = 128
UNROLL1, UNROLL2, UNROLL3, UNROLL4, FUSED = 16, 64, 32, 8, 4
BF = jnp.bfloat16
F32 = jnp.float32
NT = (((1,), (1,)), ((), ()))
TN = (((0,), (0,)), ((), ()))


def iota(shape, axis):
    return lax.broadcasted_iota(jnp.int32, shape, axis)


def small(ints):
    return ints.astype(F32).astype(BF)


def copy_in(pairs, sem):
    copies = [pltpu.make_async_copy(src, dst, sem.at[i]) for i, (src, dst) in enumerate(pairs)]
    for c in copies:
        c.start()
    return copies


def invert_kernel(place_ref, perm_hbm, sign_hbm, rows_hbm, out_hbm, perm_ref, sign_ref, rows_ref, send_ref, sem):
    for c in copy_in(((perm_hbm, perm_ref), (sign_hbm, sign_ref), (rows_hbm, rows_ref)), sem):
        c.wait()
    spot = perm_ref[...] & (SECTION - 1)
    group_of = SECTION // LANES
    row = iota((2 * group_of, SECTION), 0)
    position = iota((2 * group_of, SECTION), 1)
    negative = (sign_ref[...] < 0).astype(jnp.int32)
    digit = jnp.where(row < group_of, position % LANES, position // LANES + group_of * negative)
    digit = jnp.where(spot // LANES == row % group_of, digit, 0)
    hot = jnp.where(small(spot % LANES) == small(iota((LANES, SECTION), 0)), jnp.array(1, BF), jnp.array(0, BF))
    found = lax.dot_general(small(digit), hot, NT, preferred_element_type=F32).astype(jnp.int32)
    code = found[:group_of] + LANES * found[group_of:]
    rows = jnp.concatenate([rows_ref[...] & (SECTION - 1)] * 4, axis=1)
    mine = jnp.where(iota((1, LANES), 1) // 32 == place_ref[0], rows, 0)
    count = send_ref.shape[0]
    for h in range(group_of):
        send_ref[:, :, h * LANES : (h + 1) * LANES] = jnp.broadcast_to(code[h : h + 1][None], (count, 1, LANES))
    send_ref[:, :, SECTION:] = jnp.broadcast_to(mine[None], (count, 1, LANES))
    total = out_hbm.shape[0] // count
    copies = copy_in([(send_ref, out_hbm.at[pl.ds(i * count, count)]) for i in range(total)], sem)
    for c in copies:
        c.wait()


def ready_kernel(
    place_ref, dos_hbm, slot_hbm, cen_hbm, scl_hbm, proj_hbm, x0, x1, out_hbm, gain_ref, sp_ref,
    dos, xs, slot_ref, cen_ref, scl_ref, proj_ref, sem,
):
    chunks = dos.shape[0]
    per = xs.shape[1]
    width = per * SECTION
    pairs = [(slot_hbm, slot_ref), (cen_hbm, cen_ref), (scl_hbm, scl_ref)]
    pairs += [(dos_hbm.at[:, pl.ds(c * width, width)], dos.at[c]) for c in range(chunks)]
    copies = copy_in(pairs + [(proj_hbm, proj_ref)], sem)
    for c in copies[:3]:
        c.wait()
    mine = jnp.broadcast_to(slot_ref[...], (CAP, V)) == iota((CAP, V), 0) + place_ref[0] * CAP
    center = jnp.sum(jnp.where(mine, jnp.broadcast_to(cen_ref[...], (CAP, V)), 0.0), axis=1, keepdims=True)
    scale = jnp.sum(jnp.where(mine, jnp.broadcast_to(scl_ref[...], (CAP, V)), 0.0), axis=1, keepdims=True)
    gain_ref[...] = jnp.broadcast_to(scale, (CAP, LANES))
    sends = []
    for c in range(chunks):
        copies[3 + c].wait()
        half, quarter = divmod(c, 4)
        spot = 2 * half + quarter - 2
        for i in range(per):
            shifted = (dos[c, :, i * SECTION : (i + 1) * SECTION].astype(F32) - center).astype(BF)
            if quarter < 2:
                (x0, x1)[quarter][half, i] = shifted
            else:
                xs[spot, i] = shifted
        if quarter >= 2:
            sends.append(pltpu.make_async_copy(xs.at[spot], out_hbm.at[pl.ds(spot * per, per)], sem.at[c]))
            sends[-1].start()
    copies[-1].wait()

    slot = slot_ref[...]
    base = sp_ref.shape[0] - 32
    target = jnp.where(slot % CAP < 32, (slot // 16 % 2) * (base // 2) + slot // CAP * 16 + slot % 16, base + slot % 32)
    for start in range(0, sp_ref.shape[0], LOW):
        rows = min(LOW, sp_ref.shape[0] - start)
        hot = (jnp.broadcast_to(target, (rows, V)) == iota((rows, V), 0) + start).astype(F32).astype(BF)
        sp_ref[start : start + rows] = jnp.dot(hot, proj_ref[...], preferred_element_type=F32).astype(BF)
    for c in sends:
        c.wait()


def butterflies(vals, step):
    while step < len(vals):
        pairs = {b: (vals[b] + vals[b + step], vals[b] - vals[b + step]) for b in range(len(vals)) if not b & step}
        vals = [pairs[b & ~step][1 if b & step else 0] for b in range(len(vals))]
        step *= 2
    return vals


def mix_kernel(place_ref, x0, x1, xs_hbm, got_ref, gain_ref, out_ref, xs_ref, spots, sem):
    blocks = spots.shape[0]
    far = UNROLL1 // 2
    group = place_ref[0]

    def fetch(b):
        return pltpu.make_async_copy(xs_hbm.at[pl.ds(b * far, far)], xs_ref.at[pl.ds(b * far, far)], sem.at[b])

    for b in range(blocks // UNROLL1):
        fetch(b).start()
    norm = 1.0 / math.sqrt(SECTION * blocks * 4)
    one, zero = jnp.array(1, BF), jnp.array(0, BF)

    def table(row):
        def signs(bits):
            bits = jnp.broadcast_to(bits, (16, LANES)) & iota((16, LANES), 0)
            bits = bits ^ (bits >> 2)
            bits = bits ^ (bits >> 1)
            return (1 - 2 * (bits & 1)).astype(F32)

        upper = signs((row >> 4) & 15)
        lower = signs(row & 15).astype(BF)
        return jnp.concatenate(
            [jnp.broadcast_to(upper[k : k + 1], (16, LANES)).astype(BF) * lower for k in range(16)], axis=0
        )

    def place(i, carry):
        fetch(i).wait()
        held = []
        for u in range(UNROLL1):
            b = i * UNROLL1 + u
            code = got_ref[group * blocks + b, :, 0:SECTION]
            low = jnp.broadcast_to(small(code & (LOW - 1)), (LOW, SECTION))
            flip = jnp.broadcast_to(small(1 - 2 * (code // SECTION)), (LOW, SECTION))
            high = jnp.broadcast_to(small((code // LOW) & (HIGH - 1)), (CAP, SECTION))
            shifted = (x0, x1)[u // 4][i, u % 4] if u < far else xs_ref[i * far + u - far]
            parts = [jnp.where(high == jnp.array(h, BF), shifted, zero) for h in range(HIGH)]
            hot = jnp.where(low == small(iota((LOW, SECTION), 0)), flip, zero)
            spot = lax.dot_general(jnp.concatenate(parts, axis=0), hot, NT, preferred_element_type=F32)
            held.append(spot)
            if len(held) == FUSED:
                held = butterflies(held, 1)
                for v in range(FUSED):
                    spots[b - FUSED + 1 + v] = held[v]
                held = []
        return carry

    lax.fori_loop(0, blocks // UNROLL1, place, 0)

    def cross(i, carry):
        rows = pl.ds(pl.multiple_of(i // (LOW // LANES) * 8, 8), 8)
        cols = pl.ds(pl.multiple_of(i % (LOW // LANES) * LANES, LANES), LANES)
        vals = butterflies([spots[b, rows, cols] for b in range(blocks)], FUSED)
        for b in range(blocks):
            spots[b, rows, cols] = vals[b]
        return carry

    lax.fori_loop(0, HIGH * CAP // 8 * (LOW // LANES), cross, 0, unroll=UNROLL2)

    lane = iota((16, LANES), 1) // 32
    gain = gain_ref[...] * norm

    def sample(d, carry):
        row = sum(got_ref[g * blocks + d, :, SECTION:] for g in range(4))
        raw = jnp.dot(spots[d].astype(BF), table(row), preferred_element_type=F32)
        parts = [raw[h * CAP : (h + 1) * CAP] for h in range(HIGH)]
        top = row // LOW
        while len(parts) > 1:
            sign = (1 - 2 * (top & 1)).astype(F32)
            parts = [parts[i] + sign * parts[i + 1] for i in range(0, len(parts), 2)]
            top = top // 2
        w = parts[0] * gain
        spun = [w[16 * q : 16 * q + 16] for q in range(4)]
        spun = [spun[0]] + [pltpu.roll(spun[q], 32 * q, 1) for q in range(1, 4)]
        for g in range(4):
            out = spun[0]
            for q in range(1, 4):
                out = jnp.where(lane == (g + q) % 4, spun[q], out)
            out_ref[g, d] = out.astype(BF)
        return carry

    lax.fori_loop(0, blocks, sample, 0, unroll=UNROLL3)


def finish_kernel(place_ref, got_ref, proj_ref, out_ref):
    files = got_ref.shape[1]
    group = place_ref[0]
    odd1 = (1 - 2 * (group % 2)).astype(F32)
    odd2 = (1 - 2 * (group // 2)).astype(F32)
    g = [got_ref[i].astype(F32) for i in range(4)]
    total = (g[0] + odd1 * g[1]) + odd2 * (g[2] + odd1 * g[3])
    total = total.reshape(files * 16, 128).astype(BF)
    half = files * 16
    out = None
    for l in range(4):
        rows = slice(32 * l, 32 * l + 32)
        q = (l + 4 - group) % 4
        low = proj_ref[pl.ds(pl.multiple_of(q % 2 * half, 16), half)]
        last = proj_ref[pl.ds(pl.multiple_of(2 * half + q % 2 * 16, 16), 16)]
        first = lax.dot_general(total, low, TN, preferred_element_type=F32)[rows]
        extra = lax.dot_general(total[half - 16 :], last, TN, preferred_element_type=F32)[rows]
        part = jnp.where(q < 2, first, extra)
        out = part if out is None else out + part
    out_ref[...] = out


def vmem(n):
    return [pl.BlockSpec(memory_space=pltpu.VMEM)] * n


def limit(mib):
    return pltpu.CompilerParams(vmem_limit_bytes=mib << 20)


def hbm(n):
    return [pl.BlockSpec(memory_space=pltpu.HBM)] * n


def stay(*arrays):
    return [pltpu.with_memory_space_constraint(a, pltpu.HBM) for a in arrays]


def smem():
    return pl.BlockSpec(memory_space=pltpu.SMEM)


def on_device(
    dosage, variant_slot, center, variant_scale, sample_signs, sample_perm, sample_rows, projection
):
    groups, devs = lax.axis_size("grp"), lax.axis_size("dev")
    both = ("grp", "dev")
    group, dev = lax.axis_index("grp"), lax.axis_index("dev")
    send = pl.pallas_call(
        invert_kernel,
        out_shape=jax.ShapeDtypeStruct((groups * devs, 1, SECTION + LANES), jnp.int32),
        in_specs=[smem()] + hbm(3),
        out_specs=hbm(1)[0],
        scratch_shapes=[
            pltpu.VMEM((1, SECTION), jnp.int32),
            pltpu.VMEM((1, SECTION), jnp.int32),
            pltpu.VMEM((1, 32), jnp.int32),
            pltpu.VMEM((8, 1, SECTION + LANES), jnp.int32),
            pltpu.SemaphoreType.DMA((groups * devs // 8,)),
        ],
        compiler_params=limit(8),
    )(group[None], *stay(sample_perm[None], sample_signs[None], sample_rows[None]))
    chunks = 8
    per = devs // chunks
    x0, x1, xs, gain, slot_proj = pl.pallas_call(
        ready_kernel,
        out_shape=(
            jax.ShapeDtypeStruct((2, per, CAP, SECTION), BF),
            jax.ShapeDtypeStruct((2, per, CAP, SECTION), BF),
            pltpu.HBM((devs // 2, CAP, SECTION), BF),
            jax.ShapeDtypeStruct((CAP, LANES), F32),
            jax.ShapeDtypeStruct((devs * 32 + 32, K), BF),
        ),
        in_specs=[smem()] + hbm(5),
        out_specs=tuple(vmem(2) + hbm(1) + vmem(2)),
        scratch_shapes=[
            pltpu.VMEM((chunks, CAP, per * SECTION), BF),
            pltpu.VMEM((chunks // 2, per, CAP, SECTION), BF),
            pltpu.VMEM((1, V), jnp.int32),
            pltpu.VMEM((1, V), F32),
            pltpu.VMEM((1, V), F32),
            pltpu.VMEM((V, K), BF),
            pltpu.SemaphoreType.DMA((chunks + 4,)),
        ],
        compiler_params=limit(16),
    )(dev[None], *stay(dosage, variant_slot[None], center[None], variant_scale[None], projection))
    got = lax.all_to_all(send, both, 0, 0, tiled=True)
    mixed = pl.pallas_call(
        mix_kernel,
        out_shape=jax.ShapeDtypeStruct((groups, devs, 16, LANES), BF),
        in_specs=[smem()] + vmem(2) + hbm(1) + vmem(2),
        out_specs=pl.BlockSpec(memory_space=pltpu.VMEM),
        compiler_params=limit(24),
        scratch_shapes=[
            pltpu.VMEM((devs // 2, CAP, SECTION), BF),
            pltpu.VMEM((devs, HIGH * CAP, LOW), F32),
            pltpu.SemaphoreType.DMA((devs,)),
        ],
    )(group[None], x0, x1, *stay(xs), got, gain)
    mixed = mixed.reshape(groups * devs, 16, 128)
    got = lax.all_to_all(mixed, both, 0, 0, tiled=True).reshape(groups, devs, 16, 128)
    return pl.pallas_call(
        finish_kernel,
        out_shape=jax.ShapeDtypeStruct((32, K), F32),
        in_specs=[smem()] + vmem(2),
        out_specs=pl.BlockSpec(memory_space=pltpu.VMEM),
        compiler_params=limit(8),
    )(group[None], got, slot_proj)


def solution(mesh):
    return jax.shard_map(
        on_device,
        mesh=mesh,
        in_specs=(
            P("dev", "grp"),
            P(),
            P(),
            P(),
            P(("grp", "dev")),
            P(("grp", "dev")),
            P(("grp", "dev")),
            P(),
        ),
        out_specs=P(("grp", "dev"), None),
        check_vma=False,
    )
```

```python
import math

import jax
import jax.numpy as jnp
from jax import lax
from jax.experimental import pallas as pl
from jax.experimental.pallas import tpu as pltpu
from jax.sharding import PartitionSpec as P

V = 1024
K = 256
SECTION = 1024
LOW = 256
HIGH = SECTION // LOW
CAP = 64
LANES = 128
UNROLL1, UNROLL2, UNROLL3, UNROLL4, FUSED = 16, 64, 32, 8, 4
BF = jnp.bfloat16
F32 = jnp.float32
NT = (((1,), (1,)), ((), ()))
TN = (((0,), (0,)), ((), ()))


def iota(shape, axis):
    return lax.broadcasted_iota(jnp.int32, shape, axis)


def small(ints):
    return ints.astype(F32).astype(BF)


def copy_in(pairs, sem):
    copies = [pltpu.make_async_copy(src, dst, sem.at[i]) for i, (src, dst) in enumerate(pairs)]
    for c in copies:
        c.start()
    return copies


def invert_kernel(place_ref, perm_hbm, sign_hbm, rows_hbm, out_hbm, perm_ref, sign_ref, rows_ref, send_ref, sem):
    for c in copy_in(((perm_hbm, perm_ref), (sign_hbm, sign_ref), (rows_hbm, rows_ref)), sem):
        c.wait()
    spot = perm_ref[...] & (SECTION - 1)
    group_of = SECTION // LANES
    row = iota((2 * group_of, SECTION), 0)
    position = iota((2 * group_of, SECTION), 1)
    negative = (sign_ref[...] < 0).astype(jnp.int32)
    digit = jnp.where(row < group_of, position % LANES, position // LANES + group_of * negative)
    digit = jnp.where(spot // LANES == row % group_of, digit, 0)
    hot = jnp.where(small(spot % LANES) == small(iota((LANES, SECTION), 0)), jnp.array(1, BF), jnp.array(0, BF))
    found = lax.dot_general(small(digit), hot, NT, preferred_element_type=F32).astype(jnp.int32)
    code = found[:group_of] + LANES * found[group_of:]
    rows = jnp.concatenate([rows_ref[...] & (SECTION - 1)] * 4, axis=1)
    mine = jnp.where(iota((1, LANES), 1) // 32 == place_ref[0], rows, 0)
    count = send_ref.shape[0]
    for h in range(group_of):
        send_ref[:, :, h * LANES : (h + 1) * LANES] = jnp.broadcast_to(code[h : h + 1][None], (count, 1, LANES))
    send_ref[:, :, SECTION:] = jnp.broadcast_to(mine[None], (count, 1, LANES))
    total = out_hbm.shape[0] // count
    copies = copy_in([(send_ref, out_hbm.at[pl.ds(i * count, count)]) for i in range(total)], sem)
    for c in copies:
        c.wait()


def ready_kernel(
    place_ref, dos_hbm, slot_hbm, cen_hbm, scl_hbm, proj_hbm, x0, x1, out_hbm, gain_ref, sp_ref,
    dos, xs, slot_ref, cen_ref, scl_ref, proj_ref, sem,
):
    chunks = dos.shape[0]
    per = xs.shape[1]
    width = per * SECTION
    pairs = [(slot_hbm, slot_ref), (cen_hbm, cen_ref), (scl_hbm, scl_ref)]
    pairs += [(dos_hbm.at[:, pl.ds(c * width, width)], dos.at[c]) for c in range(chunks)]
    copies = copy_in(pairs + [(proj_hbm, proj_ref)], sem)
    for c in copies[:3]:
        c.wait()
    mine = jnp.broadcast_to(slot_ref[...], (CAP, V)) == iota((CAP, V), 0) + place_ref[0] * CAP
    center = jnp.sum(jnp.where(mine, jnp.broadcast_to(cen_ref[...], (CAP, V)), 0.0), axis=1, keepdims=True)
    scale = jnp.sum(jnp.where(mine, jnp.broadcast_to(scl_ref[...], (CAP, V)), 0.0), axis=1, keepdims=True)
    gain_ref[...] = jnp.broadcast_to(scale, (CAP, LANES))
    sends = []
    for c in range(chunks):
        copies[3 + c].wait()
        half, quarter = divmod(c, 4)
        spot = 2 * half + quarter - 2
        for i in range(per):
            shifted = (dos[c, :, i * SECTION : (i + 1) * SECTION].astype(F32) - center).astype(BF)
            if quarter < 2:
                (x0, x1)[quarter][half, i] = shifted
            else:
                xs[spot, i] = shifted
        if quarter >= 2:
            sends.append(pltpu.make_async_copy(xs.at[spot], out_hbm.at[pl.ds(spot * per, per)], sem.at[c]))
            sends[-1].start()
    copies[-1].wait()

    slot = slot_ref[...]
    base = sp_ref.shape[0] - 32
    target = jnp.where(slot % CAP < 32, (slot // 16 % 2) * (base // 2) + slot // CAP * 16 + slot % 16, base + slot % 32)
    for start in range(0, sp_ref.shape[0], LOW):
        rows = min(LOW, sp_ref.shape[0] - start)
        hot = (jnp.broadcast_to(target, (rows, V)) == iota((rows, V), 0) + start).astype(F32).astype(BF)
        sp_ref[start : start + rows] = jnp.dot(hot, proj_ref[...], preferred_element_type=F32).astype(BF)
    for c in sends:
        c.wait()


def butterflies(vals, step):
    while step < len(vals):
        pairs = {b: (vals[b] + vals[b + step], vals[b] - vals[b + step]) for b in range(len(vals)) if not b & step}
        vals = [pairs[b & ~step][1 if b & step else 0] for b in range(len(vals))]
        step *= 2
    return vals


def mix_kernel(place_ref, x0, x1, xs_hbm, got_ref, gain_ref, out_ref, xs_ref, spots, sem):
    blocks = spots.shape[0]
    far = UNROLL1 // 2
    group = place_ref[0]

    def fetch(b):
        return pltpu.make_async_copy(xs_hbm.at[pl.ds(b * far, far)], xs_ref.at[pl.ds(b * far, far)], sem.at[b])

    for b in range(blocks // UNROLL1):
        fetch(b).start()
    norm = 1.0 / math.sqrt(SECTION * blocks * 4)
    one, zero = jnp.array(1, BF), jnp.array(0, BF)

    def table(row):
        def signs(bits):
            bits = jnp.broadcast_to(bits, (16, LANES)) & iota((16, LANES), 0)
            bits = bits ^ (bits >> 2)
            bits = bits ^ (bits >> 1)
            return (1 - 2 * (bits & 1)).astype(F32)

        upper = signs((row >> 4) & 15)
        lower = signs(row & 15).astype(BF)
        return jnp.concatenate(
            [jnp.broadcast_to(upper[k : k + 1], (16, LANES)).astype(BF) * lower for k in range(16)], axis=0
        )

    def place(i, carry):
        fetch(i).wait()
        held = []
        for u in range(UNROLL1):
            b = i * UNROLL1 + u
            code = got_ref[group * blocks + b, :, 0:SECTION]
            low = jnp.broadcast_to(small(code & (LOW - 1)), (LOW, SECTION))
            flip = jnp.broadcast_to(small(1 - 2 * (code // SECTION)), (LOW, SECTION))
            high = jnp.broadcast_to(small((code // LOW) & (HIGH - 1)), (CAP, SECTION))
            shifted = (x0, x1)[u // 4][i, u % 4] if u < far else xs_ref[i * far + u - far]
            parts = [jnp.where(high == jnp.array(h, BF), shifted, zero) for h in range(HIGH)]
            hot = jnp.where(low == small(iota((LOW, SECTION), 0)), flip, zero)
            spot = lax.dot_general(jnp.concatenate(parts, axis=0), hot, NT, preferred_element_type=F32)
            held.append(spot)
            if len(held) == FUSED:
                held = butterflies(held, 1)
                for v in range(FUSED):
                    spots[b - FUSED + 1 + v] = held[v]
                held = []
        return carry

    lax.fori_loop(0, blocks // UNROLL1, place, 0)

    def cross(i, carry):
        rows = pl.ds(pl.multiple_of(i // (LOW // LANES) * 8, 8), 8)
        cols = pl.ds(pl.multiple_of(i % (LOW // LANES) * LANES, LANES), LANES)
        vals = butterflies([spots[b, rows, cols] for b in range(blocks)], FUSED)
        for b in range(blocks):
            spots[b, rows, cols] = vals[b]
        return carry

    lax.fori_loop(0, HIGH * CAP // 8 * (LOW // LANES), cross, 0, unroll=UNROLL2)

    lane = iota((16, LANES), 1) // 32
    gain = gain_ref[...] * norm

    def sample(d, carry):
        row = sum(got_ref[g * blocks + d, :, SECTION:] for g in range(4))
        raw = jnp.dot(spots[d].astype(BF), table(row), preferred_element_type=F32)
        parts = [raw[h * CAP : (h + 1) * CAP] for h in range(HIGH)]
        top = row // LOW
        while len(parts) > 1:
            sign = (1 - 2 * (top & 1)).astype(F32)
            parts = [parts[i] + sign * parts[i + 1] for i in range(0, len(parts), 2)]
            top = top // 2
        w = parts[0] * gain
        spun = [w[16 * q : 16 * q + 16] for q in range(4)]
        spun = [spun[0]] + [pltpu.roll(spun[q], 32 * q, 1) for q in range(1, 4)]
        for g in range(4):
            out = spun[0]
            for q in range(1, 4):
                out = jnp.where(lane == (g + q) % 4, spun[q], out)
            out_ref[g, d] = out.astype(BF)
        return carry

    lax.fori_loop(0, blocks, sample, 0, unroll=UNROLL3)


def finish_kernel(place_ref, got_ref, proj_ref, out_ref, full):
    files = got_ref.shape[1]
    group = place_ref[0]
    odd1 = (1 - 2 * (group % 2)).astype(F32)
    odd2 = (1 - 2 * (group // 2)).astype(F32)
    g = [got_ref[i].astype(F32) for i in range(4)]
    total = (g[0] + odd1 * g[1]) + odd2 * (g[2] + odd1 * g[3])
    total = total.reshape(files * 16, 128).astype(BF)
    half = files * 16
    for q in range(4):
        lhs = total if q < 2 else total[half - 16 :]
        rhs = proj_ref[q * half : (q + 1) * half] if q < 2 else proj_ref[2 * half + (q - 2) * 16 : 2 * half + (q - 1) * 16]
        full[q] = lax.dot_general(lhs, rhs, TN, preferred_element_type=F32)
    out = None
    for q in range(4):
        part = full[q, pl.ds(pl.multiple_of((q + group) % 4 * 32, 32), 32)]
        out = part if out is None else out + part
    out_ref[...] = out


def vmem(n):
    return [pl.BlockSpec(memory_space=pltpu.VMEM)] * n


def limit(mib):
    return pltpu.CompilerParams(vmem_limit_bytes=mib << 20)


def hbm(n):
    return [pl.BlockSpec(memory_space=pltpu.HBM)] * n


def stay(*arrays):
    return [pltpu.with_memory_space_constraint(a, pltpu.HBM) for a in arrays]


def smem():
    return pl.BlockSpec(memory_space=pltpu.SMEM)


def on_device(
    dosage, variant_slot, center, variant_scale, sample_signs, sample_perm, sample_rows, projection
):
    groups, devs = lax.axis_size("grp"), lax.axis_size("dev")
    both = ("grp", "dev")
    group, dev = lax.axis_index("grp"), lax.axis_index("dev")
    send = pl.pallas_call(
        invert_kernel,
        out_shape=jax.ShapeDtypeStruct((groups * devs, 1, SECTION + LANES), jnp.int32),
        in_specs=[smem()] + hbm(3),
        out_specs=hbm(1)[0],
        scratch_shapes=[
            pltpu.VMEM((1, SECTION), jnp.int32),
            pltpu.VMEM((1, SECTION), jnp.int32),
            pltpu.VMEM((1, 32), jnp.int32),
            pltpu.VMEM((16, 1, SECTION + LANES), jnp.int32),
            pltpu.SemaphoreType.DMA((groups * devs // 16,)),
        ],
        compiler_params=limit(8),
    )(group[None], *stay(sample_perm[None], sample_signs[None], sample_rows[None]))
    chunks = 8
    per = devs // chunks
    x0, x1, xs, gain, slot_proj = pl.pallas_call(
        ready_kernel,
        out_shape=(
            jax.ShapeDtypeStruct((2, per, CAP, SECTION), BF),
            jax.ShapeDtypeStruct((2, per, CAP, SECTION), BF),
            pltpu.HBM((devs // 2, CAP, SECTION), BF),
            jax.ShapeDtypeStruct((CAP, LANES), F32),
            jax.ShapeDtypeStruct((devs * 32 + 32, K), BF),
        ),
        in_specs=[smem()] + hbm(5),
        out_specs=tuple(vmem(2) + hbm(1) + vmem(2)),
        scratch_shapes=[
            pltpu.VMEM((chunks, CAP, per * SECTION), BF),
            pltpu.VMEM((chunks // 2, per, CAP, SECTION), BF),
            pltpu.VMEM((1, V), jnp.int32),
            pltpu.VMEM((1, V), F32),
            pltpu.VMEM((1, V), F32),
            pltpu.VMEM((V, K), BF),
            pltpu.SemaphoreType.DMA((chunks + 4,)),
        ],
        compiler_params=limit(16),
    )(dev[None], *stay(dosage, variant_slot[None], center[None], variant_scale[None], projection))
    got = lax.all_to_all(send, both, 0, 0, tiled=True)
    mixed = pl.pallas_call(
        mix_kernel,
        out_shape=jax.ShapeDtypeStruct((groups, devs, 16, LANES), BF),
        in_specs=[smem()] + vmem(2) + hbm(1) + vmem(2),
        out_specs=pl.BlockSpec(memory_space=pltpu.VMEM),
        compiler_params=limit(24),
        scratch_shapes=[
            pltpu.VMEM((devs // 2, CAP, SECTION), BF),
            pltpu.VMEM((devs, HIGH * CAP, LOW), F32),
            pltpu.SemaphoreType.DMA((devs,)),
        ],
    )(group[None], x0, x1, *stay(xs), got, gain)
    mixed = mixed.reshape(groups * devs, 16, 128)
    got = lax.all_to_all(mixed, both, 0, 0, tiled=True).reshape(groups, devs, 16, 128)
    return pl.pallas_call(
        finish_kernel,
        out_shape=jax.ShapeDtypeStruct((32, K), F32),
        in_specs=[smem()] + vmem(2),
        out_specs=pl.BlockSpec(memory_space=pltpu.VMEM),
        scratch_shapes=[pltpu.VMEM((4, 4 * 32, K), F32)],
        compiler_params=limit(8),
    )(group[None], got, slot_proj)


def solution(mesh):
    return jax.shard_map(
        on_device,
        mesh=mesh,
        in_specs=(
            P("dev", "grp"),
            P(),
            P(),
            P(),
            P(("grp", "dev")),
            P(("grp", "dev")),
            P(("grp", "dev")),
            P(),
        ),
        out_specs=P(("grp", "dev"), None),
        check_vma=False,
    )
```

```python
import math

import jax
import jax.numpy as jnp
from jax import lax
from jax.experimental import pallas as pl
from jax.experimental.pallas import tpu as pltpu
from jax.sharding import PartitionSpec as P

V = 1024
K = 256
SECTION = 1024
LOW = 256
HIGH = SECTION // LOW
CAP = 64
LANES = 128
UNROLL1, UNROLL2, UNROLL3, UNROLL4, FUSED = 16, 64, 32, 8, 8
BF = jnp.bfloat16
F32 = jnp.float32
NT = (((1,), (1,)), ((), ()))
TN = (((0,), (0,)), ((), ()))


def iota(shape, axis):
    return lax.broadcasted_iota(jnp.int32, shape, axis)


def small(ints):
    return ints.astype(F32).astype(BF)


def copy_in(pairs, sem):
    copies = [pltpu.make_async_copy(src, dst, sem.at[i]) for i, (src, dst) in enumerate(pairs)]
    for c in copies:
        c.start()
    return copies


def invert_kernel(place_ref, perm_hbm, sign_hbm, rows_hbm, out_hbm, perm_ref, sign_ref, rows_ref, send_ref, sem):
    for c in copy_in(((perm_hbm, perm_ref), (sign_hbm, sign_ref), (rows_hbm, rows_ref)), sem):
        c.wait()
    spot = perm_ref[...] & (SECTION - 1)
    group_of = SECTION // LANES
    row = iota((2 * group_of, SECTION), 0)
    position = iota((2 * group_of, SECTION), 1)
    negative = (sign_ref[...] < 0).astype(jnp.int32)
    digit = jnp.where(row < group_of, position % LANES, position // LANES + group_of * negative)
    digit = jnp.where(spot // LANES == row % group_of, digit, 0)
    hot = jnp.where(small(spot % LANES) == small(iota((LANES, SECTION), 0)), jnp.array(1, BF), jnp.array(0, BF))
    found = lax.dot_general(small(digit), hot, NT, preferred_element_type=F32).astype(jnp.int32)
    code = found[:group_of] + LANES * found[group_of:]
    rows = jnp.concatenate([rows_ref[...] & (SECTION - 1)] * 4, axis=1)
    mine = jnp.where(iota((1, LANES), 1) // 32 == place_ref[0], rows, 0)
    count = send_ref.shape[0]
    for h in range(group_of):
        send_ref[:, :, h * LANES : (h + 1) * LANES] = jnp.broadcast_to(code[h : h + 1][None], (count, 1, LANES))
    send_ref[:, :, SECTION:] = jnp.broadcast_to(mine[None], (count, 1, LANES))
    total = out_hbm.shape[0] // count
    copies = copy_in([(send_ref, out_hbm.at[pl.ds(i * count, count)]) for i in range(total)], sem)
    for c in copies:
        c.wait()


def ready_kernel(
    place_ref, dos_hbm, slot_hbm, cen_hbm, scl_hbm, proj_hbm, x0, x1, out_hbm, gain_ref, sp_ref,
    dos, xs, slot_ref, cen_ref, scl_ref, proj_ref, sem,
):
    chunks = dos.shape[0]
    per = xs.shape[1]
    width = per * SECTION
    pairs = [(slot_hbm, slot_ref), (cen_hbm, cen_ref), (scl_hbm, scl_ref)]
    pairs += [(dos_hbm.at[:, pl.ds(c * width, width)], dos.at[c]) for c in range(chunks)]
    copies = copy_in(pairs + [(proj_hbm, proj_ref)], sem)
    for c in copies[:3]:
        c.wait()
    mine = jnp.broadcast_to(slot_ref[...], (CAP, V)) == iota((CAP, V), 0) + place_ref[0] * CAP
    center = jnp.sum(jnp.where(mine, jnp.broadcast_to(cen_ref[...], (CAP, V)), 0.0), axis=1, keepdims=True)
    scale = jnp.sum(jnp.where(mine, jnp.broadcast_to(scl_ref[...], (CAP, V)), 0.0), axis=1, keepdims=True)
    gain_ref[...] = jnp.broadcast_to(scale, (CAP, LANES))
    sends = []
    for c in range(chunks):
        copies[3 + c].wait()
        half, quarter = divmod(c, 4)
        spot = 2 * half + quarter - 2
        for i in range(per):
            shifted = (dos[c, :, i * SECTION : (i + 1) * SECTION].astype(F32) - center).astype(BF)
            if quarter < 2:
                (x0, x1)[quarter][half, i] = shifted
            else:
                xs[spot, i] = shifted
        if quarter >= 2:
            sends.append(pltpu.make_async_copy(xs.at[spot], out_hbm.at[pl.ds(spot * per, per)], sem.at[c]))
            sends[-1].start()
    copies[-1].wait()

    slot = slot_ref[...]
    base = sp_ref.shape[0] - 32
    target = jnp.where(slot % CAP < 32, (slot // 16 % 2) * (base // 2) + slot // CAP * 16 + slot % 16, base + slot % 32)
    for start in range(0, sp_ref.shape[0], LOW):
        rows = min(LOW, sp_ref.shape[0] - start)
        hot = (jnp.broadcast_to(target, (rows, V)) == iota((rows, V), 0) + start).astype(F32).astype(BF)
        sp_ref[start : start + rows] = jnp.dot(hot, proj_ref[...], preferred_element_type=F32).astype(BF)
    for c in sends:
        c.wait()


def butterflies(vals, step):
    while step < len(vals):
        pairs = {b: (vals[b] + vals[b + step], vals[b] - vals[b + step]) for b in range(len(vals)) if not b & step}
        vals = [pairs[b & ~step][1 if b & step else 0] for b in range(len(vals))]
        step *= 2
    return vals


def mix_kernel(place_ref, x0, x1, xs_hbm, got_ref, gain_ref, out_ref, xs_ref, spots, sem):
    blocks = spots.shape[0]
    far = UNROLL1 // 2
    group = place_ref[0]

    def fetch(b):
        return pltpu.make_async_copy(xs_hbm.at[pl.ds(b * far, far)], xs_ref.at[pl.ds(b * far, far)], sem.at[b])

    for b in range(blocks // UNROLL1):
        fetch(b).start()
    norm = 1.0 / math.sqrt(SECTION * blocks * 4)
    one, zero = jnp.array(1, BF), jnp.array(0, BF)

    def table(row):
        def signs(bits):
            bits = jnp.broadcast_to(bits, (16, LANES)) & iota((16, LANES), 0)
            bits = bits ^ (bits >> 2)
            bits = bits ^ (bits >> 1)
            return (1 - 2 * (bits & 1)).astype(F32)

        upper = signs((row >> 4) & 15)
        lower = signs(row & 15).astype(BF)
        return jnp.concatenate(
            [jnp.broadcast_to(upper[k : k + 1], (16, LANES)).astype(BF) * lower for k in range(16)], axis=0
        )

    def place(i, carry):
        fetch(i).wait()
        held = []
        for u in range(UNROLL1):
            b = i * UNROLL1 + u
            code = got_ref[group * blocks + b, :, 0:SECTION]
            low = jnp.broadcast_to(small(code & (LOW - 1)), (LOW, SECTION))
            flip = jnp.broadcast_to(small(1 - 2 * (code // SECTION)), (LOW, SECTION))
            high = jnp.broadcast_to(small((code // LOW) & (HIGH - 1)), (CAP, SECTION))
            shifted = (x0, x1)[u // 4][i, u % 4] if u < far else xs_ref[i * far + u - far]
            parts = [jnp.where(high == jnp.array(h, BF), shifted, zero) for h in range(HIGH)]
            hot = jnp.where(low == small(iota((LOW, SECTION), 0)), flip, zero)
            spot = lax.dot_general(jnp.concatenate(parts, axis=0), hot, NT, preferred_element_type=F32)
            held.append(spot)
            if len(held) == FUSED:
                held = butterflies(held, 1)
                for v in range(FUSED):
                    spots[b - FUSED + 1 + v] = held[v]
                held = []
        return carry

    lax.fori_loop(0, blocks // UNROLL1, place, 0)

    def cross(i, carry):
        rows = pl.ds(pl.multiple_of(i // (LOW // LANES) * 8, 8), 8)
        cols = pl.ds(pl.multiple_of(i % (LOW // LANES) * LANES, LANES), LANES)
        vals = butterflies([spots[b, rows, cols] for b in range(blocks)], FUSED)
        for b in range(blocks):
            spots[b, rows, cols] = vals[b]
        return carry

    lax.fori_loop(0, HIGH * CAP // 8 * (LOW // LANES), cross, 0, unroll=UNROLL2)

    lane = iota((16, LANES), 1) // 32
    gain = gain_ref[...] * norm

    def sample(d, carry):
        row = sum(got_ref[g * blocks + d, :, SECTION:] for g in range(4))
        raw = jnp.dot(spots[d].astype(BF), table(row), preferred_element_type=F32)
        parts = [raw[h * CAP : (h + 1) * CAP] for h in range(HIGH)]
        top = row // LOW
        while len(parts) > 1:
            sign = (1 - 2 * (top & 1)).astype(F32)
            parts = [parts[i] + sign * parts[i + 1] for i in range(0, len(parts), 2)]
            top = top // 2
        w = parts[0] * gain
        spun = [w[16 * q : 16 * q + 16] for q in range(4)]
        spun = [spun[0]] + [pltpu.roll(spun[q], 32 * q, 1) for q in range(1, 4)]
        for g in range(4):
            out = spun[0]
            for q in range(1, 4):
                out = jnp.where(lane == (g + q) % 4, spun[q], out)
            out_ref[g, d] = out.astype(BF)
        return carry

    lax.fori_loop(0, blocks, sample, 0, unroll=UNROLL3)


def finish_kernel(place_ref, got_ref, proj_ref, out_ref, full):
    files = got_ref.shape[1]
    group = place_ref[0]
    odd1 = (1 - 2 * (group % 2)).astype(F32)
    odd2 = (1 - 2 * (group // 2)).astype(F32)
    g = [got_ref[i].astype(F32) for i in range(4)]
    total = (g[0] + odd1 * g[1]) + odd2 * (g[2] + odd1 * g[3])
    total = total.reshape(files * 16, 128).astype(BF)
    half = files * 16
    for q in range(4):
        lhs = total if q < 2 else total[half - 16 :]
        rhs = proj_ref[q * half : (q + 1) * half] if q < 2 else proj_ref[2 * half + (q - 2) * 16 : 2 * half + (q - 1) * 16]
        full[q] = lax.dot_general(lhs, rhs, TN, preferred_element_type=F32)
    out = None
    for q in range(4):
        part = full[q, pl.ds(pl.multiple_of((q + group) % 4 * 32, 32), 32)]
        out = part if out is None else out + part
    out_ref[...] = out


def vmem(n):
    return [pl.BlockSpec(memory_space=pltpu.VMEM)] * n


def limit(mib):
    return pltpu.CompilerParams(vmem_limit_bytes=mib << 20)


def hbm(n):
    return [pl.BlockSpec(memory_space=pltpu.HBM)] * n


def stay(*arrays):
    return [pltpu.with_memory_space_constraint(a, pltpu.HBM) for a in arrays]


def smem():
    return pl.BlockSpec(memory_space=pltpu.SMEM)


def on_device(
    dosage, variant_slot, center, variant_scale, sample_signs, sample_perm, sample_rows, projection
):
    groups, devs = lax.axis_size("grp"), lax.axis_size("dev")
    both = ("grp", "dev")
    group, dev = lax.axis_index("grp"), lax.axis_index("dev")
    send = pl.pallas_call(
        invert_kernel,
        out_shape=jax.ShapeDtypeStruct((groups * devs, 1, SECTION + LANES), jnp.int32),
        in_specs=[smem()] + hbm(3),
        out_specs=hbm(1)[0],
        scratch_shapes=[
            pltpu.VMEM((1, SECTION), jnp.int32),
            pltpu.VMEM((1, SECTION), jnp.int32),
            pltpu.VMEM((1, 32), jnp.int32),
            pltpu.VMEM((16, 1, SECTION + LANES), jnp.int32),
            pltpu.SemaphoreType.DMA((groups * devs // 16,)),
        ],
        compiler_params=limit(8),
    )(group[None], *stay(sample_perm[None], sample_signs[None], sample_rows[None]))
    chunks = 8
    per = devs // chunks
    x0, x1, xs, gain, slot_proj = pl.pallas_call(
        ready_kernel,
        out_shape=(
            jax.ShapeDtypeStruct((2, per, CAP, SECTION), BF),
            jax.ShapeDtypeStruct((2, per, CAP, SECTION), BF),
            pltpu.HBM((devs // 2, CAP, SECTION), BF),
            jax.ShapeDtypeStruct((CAP, LANES), F32),
            jax.ShapeDtypeStruct((devs * 32 + 32, K), BF),
        ),
        in_specs=[smem()] + hbm(5),
        out_specs=tuple(vmem(2) + hbm(1) + vmem(2)),
        scratch_shapes=[
            pltpu.VMEM((chunks, CAP, per * SECTION), BF),
            pltpu.VMEM((chunks // 2, per, CAP, SECTION), BF),
            pltpu.VMEM((1, V), jnp.int32),
            pltpu.VMEM((1, V), F32),
            pltpu.VMEM((1, V), F32),
            pltpu.VMEM((V, K), BF),
            pltpu.SemaphoreType.DMA((chunks + 4,)),
        ],
        compiler_params=limit(16),
    )(dev[None], *stay(dosage, variant_slot[None], center[None], variant_scale[None], projection))
    got = lax.all_to_all(send, both, 0, 0, tiled=True)
    mixed = pl.pallas_call(
        mix_kernel,
        out_shape=jax.ShapeDtypeStruct((groups, devs, 16, LANES), BF),
        in_specs=[smem()] + vmem(2) + hbm(1) + vmem(2),
        out_specs=pl.BlockSpec(memory_space=pltpu.VMEM),
        compiler_params=limit(24),
        scratch_shapes=[
            pltpu.VMEM((devs // 2, CAP, SECTION), BF),
            pltpu.VMEM((devs, HIGH * CAP, LOW), F32),
            pltpu.SemaphoreType.DMA((devs,)),
        ],
    )(group[None], x0, x1, *stay(xs), got, gain)
    mixed = mixed.reshape(groups * devs, 16, 128)
    got = lax.all_to_all(mixed, both, 0, 0, tiled=True).reshape(groups, devs, 16, 128)
    return pl.pallas_call(
        finish_kernel,
        out_shape=jax.ShapeDtypeStruct((32, K), F32),
        in_specs=[smem()] + vmem(2),
        out_specs=pl.BlockSpec(memory_space=pltpu.VMEM),
        scratch_shapes=[pltpu.VMEM((4, 4 * 32, K), F32)],
        compiler_params=limit(8),
    )(group[None], got, slot_proj)


def solution(mesh):
    return jax.shard_map(
        on_device,
        mesh=mesh,
        in_specs=(
            P("dev", "grp"),
            P(),
            P(),
            P(),
            P(("grp", "dev")),
            P(("grp", "dev")),
            P(("grp", "dev")),
            P(),
        ),
        out_specs=P(("grp", "dev"), None),
        check_vma=False,
    )
```
